32 devices in a mesh: slides: 1, row: 16 (over z, y, x), col: 2 (over core).
Axes of the slice: x: 2, y: 2, z: 4, core: 2. Of those that a mesh axis runs over, the one named last changes fastest.
Arguments:
- image: bfloat16 [64, 128, 768], P(('slides', 'row'), 'col'), may hold values from -6 to 6
- dw_kernel: float32 [49, 768], replicated, may hold values from -0.875 to 0.875
- w_in: bfloat16 [768, 3072], replicated, may hold values from -0.21875 to 0.21875
- w_out: bfloat16 [3072, 768], replicated, may hold values from -0.109375 to 0.109375
- layer_scale: float32 [768], replicated, may hold values from 0.5 to 1.5
- region_ids: int32 [32, 64], P(('slides', 'row'), 'col'), may hold values from 0 to 127, as said below
- region_slot: int32 [128], P('slides'), may hold values from 0 to 127, each once
- pool_grad: bfloat16 [128, 768], P(('slides', 'row', 'col')), may hold values from -6 to 6
Outputs:
- region_pool: float32 [128, 768], P(('slides', 'row', 'col'))
- grad_image: bfloat16 [64, 128, 768], P(('slides', 'row'), 'col')
- grad_w_in: float32 [768, 3072], P('slides', ('row', 'col'))
- grad_w_out: float32 [3072, 768], P(('slides', 'row', 'col'))
- grad_kernel: float32 [49, 768], P('slides')
The draws below stay inside these ranges and needn't reach their ends.
Inputs may be any that keep to these rules, and one draw needn't show every extreme that they name: `region_ids`: every region is named by some tile. `region_slot`: each slot once; slot s lies on index s // 4 of row+col.
All inputs are finite; a program needn't handle non-finite values.
Results may differ from the reference program's by a relative error of at most 0.007.
Values may be sent and summed in bfloat16 or wider, within the bound.
No kernel may reach another device: no remote copies, remote signals or barrier semaphores. Data moves between devices by JAX's collectives and lax.ppermute only.
A program may use at most 192 MiB of HBM per device.

```python
import math
import jax
import jax.numpy as jnp
from jax import lax

C = 768
FF = 3072
ROWS = 64
COLS = 128
REGIONS = 128


def draw_region_ids(key, part):
    first, second, third = jax.random.split(key, 3)
    total = ROWS // 2 * (COLS // 2)
    lower = jax.random.randint(first, (total,), 0, REGIONS)
    upper = jax.random.randint(second, (total,), 0, REGIONS)
    order = jax.random.permutation(third, REGIONS).astype(jnp.int32)
    labels = order[jnp.minimum(lower, upper)]
    labels = labels.at[:REGIONS].set(order)
    return labels.reshape(ROWS // 2, COLS // 2).astype(jnp.int32)


def levels(key, shape, cuts, low, high):
    gain, own = 1.0, jax.random.fold_in(key, 6)
    for position, parts in cuts:
        heights = jnp.exp(jax.random.uniform(jax.random.fold_in(own, position), (parts,), jnp.float32, low / len(cuts), high / len(cuts)))
        gain = gain * jnp.repeat(heights, shape[position] // parts).reshape([-1 if axis == position else 1 for axis in range(len(shape))])
    return gain


def noise(stream_key, extent, spread, most, cuts=(), kind=jnp.bfloat16):
    loudness = levels(stream_key, extent, cuts, -0.22, 0.18) if cuts else 1.0
    entries = jax.random.normal(stream_key, extent, jnp.float32) * spread * loudness
    return jnp.minimum(jnp.maximum(entries, -most), most).astype(kind)


def setup_inputs(seed: int = 0, part: int = 0) -> dict:
    seeds = jax.random.split(jax.random.key(seed), 9)
    part_keys = jax.random.split(jax.random.fold_in(seeds[8], part), 9)
    image = noise(part_keys[0], (ROWS, COLS, C), 1.0, 6.0, ((0, 16), (1, 2)))
    dw_kernel = noise(seeds[1], (49, C), 49 ** -0.5, 0.875, (), jnp.float32)
    w_in = noise(seeds[2], (C, FF), C ** -0.5, 0.21875)
    w_out = noise(seeds[3], (FF, C), FF ** -0.5, 0.109375)
    layer_scale = jnp.clip(jax.random.uniform(seeds[4], (C,), jnp.float32, 0.5, 1.5), 0.5, 1.5)
    region_ids = draw_region_ids(jax.random.fold_in(jax.random.fold_in(seeds[8], part), 71), part)
    region_slot = jax.random.permutation(part_keys[6], REGIONS).astype(jnp.int32)
    pool_grad = noise(part_keys[7], (REGIONS, C), 1.0, 6.0, ((0, 32),))
    return {"image": image, "dw_kernel": dw_kernel, "w_in": w_in, "w_out": w_out, "layer_scale": layer_scale, "region_ids": region_ids, "region_slot": region_slot, "pool_grad": pool_grad}


def reference(image, dw_kernel, w_in, w_out, layer_scale, region_ids, region_slot, pool_grad):
    height, breadth, width = image.shape
    taps = dw_kernel.reshape(7, 7, width)
    xfull = image.astype(jnp.float32)
    xpad = jnp.pad(xfull, ((3, 3), (3, 3), (0, 0)))
    conv = jnp.zeros((height, breadth, width), jnp.float32)
    for a in range(7):
        for b in range(7):
            conv = conv + xpad[a:a + height, b:b + breadth] * taps[a, b]
    centre = conv - lax.optimization_barrier(jnp.mean(conv, axis=-1, keepdims=True))
    inv_std = lax.rsqrt(lax.optimization_barrier(jnp.mean(centre * centre, axis=-1, keepdims=True)) + 1e-06)
    normed_f = centre * inv_std
    normed = normed_f.astype(jnp.bfloat16).reshape(-1, width)
    pre = jnp.dot(normed, w_in, preferred_element_type=jnp.float32)
    hidden = jax.nn.gelu(pre, approximate=False).astype(jnp.bfloat16)
    branch = jnp.dot(hidden, w_out, preferred_element_type=jnp.float32).reshape(height, breadth, width)
    block = (xfull + layer_scale * branch).astype(jnp.bfloat16)
    tile_sum = block.astype(jnp.float32).reshape(height // 2, 2, breadth // 2, 2, width).sum(axis=(1, 3)).reshape(-1, width)
    slots = region_slot[region_ids.reshape(-1)].astype(jnp.int32)
    region_sum = jax.ops.segment_sum(tile_sum, slots, REGIONS)
    count = jax.ops.segment_sum(jnp.ones(slots.shape, jnp.float32), slots, REGIONS)
    region_pool = region_sum / (4.0 * count)[:, None]
    region_grad = (pool_grad.astype(jnp.float32) / (4.0 * count)[:, None]).astype(jnp.bfloat16)
    tile_grad = region_grad[slots].astype(jnp.float32).reshape(height // 2, 1, breadth // 2, 1, width)
    dblock = jnp.broadcast_to(tile_grad, (height // 2, 2, breadth // 2, 2, width)).reshape(height, breadth, width)
    g_out = (dblock * layer_scale).astype(jnp.bfloat16).reshape(-1, width)
    grad_w_out = jnp.dot(hidden.T, g_out, preferred_element_type=jnp.float32)
    dhidden = jnp.dot(g_out, w_out.T, preferred_element_type=jnp.float32)
    cdf = 0.5 * (1.0 + lax.erf(pre / math.sqrt(2.0)))
    density = jnp.exp(-0.5 * pre * pre) / math.sqrt(2.0 * math.pi)
    g_in = (dhidden * (cdf + pre * density)).astype(jnp.bfloat16)
    grad_w_in = jnp.dot(normed.T, g_in, preferred_element_type=jnp.float32)
    dnorm = jnp.dot(g_in, w_in.T, preferred_element_type=jnp.float32).reshape(height, breadth, width)
    dconv = inv_std * (dnorm - lax.optimization_barrier(jnp.mean(dnorm, axis=-1, keepdims=True)) - normed_f * lax.optimization_barrier(jnp.mean(dnorm * normed_f, axis=-1, keepdims=True)))
    dpad = jnp.pad(dconv, ((3, 3), (3, 3), (0, 0)))
    back = jnp.zeros((height, breadth, width), jnp.float32)
    kernel_rows = []
    for a in range(7):
        for b in range(7):
            back = back + dpad[6 - a:6 - a + height, 6 - b:6 - b + breadth] * taps[a, b]
            kernel_rows.append(lax.optimization_barrier(jnp.sum(xpad[a:a + height, b:b + breadth] * dconv, axis=(0, 1))))
    grad_kernel = jnp.stack(kernel_rows, axis=0)
    grad_image = (dblock + back).astype(jnp.bfloat16)
    return (region_pool, grad_image, grad_w_in, grad_w_out, grad_kernel)
```

```python
import math

import jax
import jax.numpy as jnp
from jax import lax
from jax.sharding import PartitionSpec as P

AXES = ("row", "col")


def exchange(value, chips, flip_core=False):
    rows = lax.axis_size("row")
    pairs = []
    for r in range(rows):
        for c in range(2):
            pairs.append((2 * r + c, 2 * (r ^ chips[c]) + (c ^ int(flip_core))))
    return lax.ppermute(value, AXES, pairs)


def swap_core(value):
    return exchange(value, (0, 0), True)


def depthwise(padded, taps, height, breadth, flipped):
    total = jnp.zeros((height, breadth, padded.shape[2]), jnp.float32)
    for a in range(7):
        if flipped:
            terms = [
                padded[6 - a : 6 - a + height, 6 - b : 6 - b + breadth] * taps[a, b]
                for b in range(7)
            ]
        else:
            terms = [padded[a : a + height, b : b + breadth] * taps[a, b] for b in range(7)]
        row_total = terms[0]
        for term in terms[1:]:
            row_total = row_total + term
        total = total + row_total
    return total


def widen(field, c):
    rows = lax.axis_size("row")
    breadth = field.shape[1]
    edge = jnp.where(c == 0, field[:, breadth - 3 :], field[:, :3])
    got = swap_core(edge)
    zero = jnp.zeros_like(got)
    wide = jnp.concatenate(
        [jnp.where(c == 0, zero, got), field, jnp.where(c == 0, got, zero)], axis=1
    )
    down = lax.ppermute(wide[-3:], "row", [(i, i + 1) for i in range(rows - 1)])
    up = lax.ppermute(wide[:3], "row", [(i + 1, i) for i in range(rows - 1)])
    return jnp.concatenate([down, wide, up], axis=0)


def layout_index(me, orders):
    bits = len(orders)
    j = jnp.arange(1 << bits, dtype=jnp.int32)
    mask = jnp.zeros_like(j)
    for k, bit in enumerate(orders):
        mask = mask | (((j >> (bits - 1 - k)) & 1) << bit)
    return me ^ mask


def shards(image, dw_kernel, w_in, w_out, layer_scale, region_ids, region_slot, pool_grad):
    height, breadth, width = image.shape
    hidden_units = w_in.shape[1]
    rows = lax.axis_size("row")
    bits = rows.bit_length() - 1
    r, c = lax.axis_index("row"), lax.axis_index("col")
    me = 2 * r + c
    half = width // 2
    regions = region_slot.shape[0]
    owned = pool_grad.shape[0]
    tiles = region_ids.size
    f32, bf16 = jnp.float32, jnp.bfloat16

    iota = jnp.arange(regions, dtype=jnp.int32)
    labels = region_ids.reshape(-1)
    slots = jnp.sum(
        jnp.where(labels[:, None] == iota[None, :], region_slot[None, :], 0), axis=1
    )
    meta = jnp.zeros((1, width), bf16)
    meta = meta.at[0, :tiles].set((slots >> 4).astype(bf16))
    meta = meta.at[0, tiles : 2 * tiles].set((slots & 15).astype(bf16))
    known = jnp.concatenate([pool_grad, meta], axis=0)[None]
    known = jnp.concatenate([known, swap_core(known)], axis=0)
    for bit in range(bits):
        known = jnp.concatenate([known, exchange(known, (1 << bit, 1 << bit))], axis=0)
    pool_xor = known[:, :owned].reshape(regions, width)
    high, low = known[:, owned, :tiles], known[:, owned, tiles : 2 * tiles]
    all_slots = (high.astype(f32) * 16.0 + low.astype(f32)).reshape(-1).astype(jnp.int32)
    device = me ^ jnp.arange(2 * rows, dtype=jnp.int32)
    xor_slot = (device[:, None] * owned + jnp.arange(owned, dtype=jnp.int32)[None]).reshape(-1)
    count = jnp.sum((all_slots[:, None] == iota[None, :]).astype(f32), axis=0)
    place = (iota[:, None] == xor_slot[None, :]).astype(bf16)
    pool_all = jnp.dot(place, pool_xor, preferred_element_type=f32)
    region_grad = (pool_all / (4.0 * count)[:, None]).astype(bf16)
    g_region = (region_grad.astype(f32) * layer_scale).astype(bf16)

    spread = jnp.broadcast_to(
        slots.reshape(height // 2, 1, breadth // 2, 1), (height // 2, 2, breadth // 2, 2)
    ).reshape(-1)
    select = (spread[:, None] == iota[None, :]).astype(bf16)

    taps = dw_kernel.reshape(7, 7, width)
    xfull = image.astype(f32)
    xpad = widen(image, c).astype(f32)
    conv = depthwise(xpad, taps, height, breadth, False)
    centre = conv - jnp.mean(conv, axis=-1, keepdims=True)
    inv_std = lax.rsqrt(jnp.mean(centre * centre, axis=-1, keepdims=True) + 1e-06)
    normed_f = centre * inv_std
    normed = normed_f.astype(bf16).reshape(-1, width)
    other_half = swap_core(lax.dynamic_slice_in_dim(normed, (1 - c) * half, half, axis=1))
    own_half = lax.dynamic_slice_in_dim(normed, c * half, half, axis=1)
    pre = jnp.dot(normed, w_in, preferred_element_type=f32)
    hidden = jax.nn.gelu(pre, approximate=False).astype(bf16)
    branch = jnp.dot(hidden, w_out, preferred_element_type=f32).reshape(height, breadth, width)
    block = (xfull + layer_scale * branch).astype(bf16).reshape(-1, width)

    order_chip = tuple(range(bits))
    chips = layout_index(r, order_chip)
    owner = jnp.concatenate([2 * chips + c, 2 * chips + (1 - c)])
    owner_slot = (owner[:, None] * owned + jnp.arange(owned, dtype=jnp.int32)[None]).reshape(-1)
    select_owner = (spread[:, None] == owner_slot[None, :]).astype(bf16)
    sums = jnp.dot(select_owner.T, block, preferred_element_type=f32)
    mid = regions // 2
    sums = sums[:mid] + swap_core(sums[mid:])
    for bit in order_chip:
        mid = mid // 2
        sums = sums[:mid] + exchange(sums[mid:], (1 << bit, 1 << bit))
    own_slot = me * owned + jnp.arange(owned, dtype=jnp.int32)
    own_count = jnp.sum((all_slots[:, None] == own_slot[None, :]).astype(f32), axis=0)
    region_pool = sums / (4.0 * own_count)[:, None]

    g_out = jnp.dot(select, g_region, preferred_element_type=f32).astype(bf16)
    dblock = jnp.dot(select, region_grad, preferred_element_type=f32).reshape(
        height, breadth, width
    )
    dhidden = jnp.dot(g_out, w_out.T, preferred_element_type=f32)
    cdf = 0.5 * (1.0 + lax.erf(pre / math.sqrt(2.0)))
    density = jnp.exp(-0.5 * pre * pre) / math.sqrt(2.0 * math.pi)
    g_in = (dhidden * (cdf + pre * density)).astype(bf16)
    g_other = swap_core(g_in)
    dims = (((0,), (0,)), ((), ()))
    grad_in = lax.dot_general(g_in, own_half, dims, preferred_element_type=f32)
    grad_in = grad_in + lax.dot_general(g_other, other_half, dims, preferred_element_type=f32)
    by_region = lax.dot_general(hidden, select, dims, preferred_element_type=f32)

    per_chip = hidden_units // rows
    per_core = per_chip // 2
    flip = [b ^ 1 if b < 2 else b for b in range(bits)]
    mine = jnp.where(c == 0, layout_index(r, order_chip), layout_index(r, flip))
    grad_in = jnp.take(grad_in.reshape(rows, per_chip, half), mine, axis=0)
    by_region = by_region.reshape(rows, 2, per_core, regions)
    h_other = swap_core(jnp.take(by_region, 1 - c, axis=1).astype(bf16))
    by_region = jnp.take(jnp.take(by_region, c, axis=1) + h_other, mine, axis=0)
    lanes, stack = regions // 128, half // 128
    packed_rows = per_core * lanes // stack
    by_region = by_region.reshape(rows, per_core, lanes, 128).transpose(0, 2, 1, 3)
    by_region = by_region.reshape(rows, stack, packed_rows, 128).transpose(0, 2, 1, 3)
    by_region = by_region.reshape(rows, packed_rows, half)
    acc = jnp.concatenate([grad_in, by_region], axis=1)
    mid = rows
    for k in range(bits):
        mid = mid // 2
        got = exchange(acc[mid:].astype(bf16), (1 << order_chip[k], 1 << flip[k]))
        acc = acc[:mid] + got
    acc = acc[0]
    grad_part = acc[:per_chip]
    grad_mine = lax.dynamic_slice_in_dim(grad_part, c * per_core, per_core, axis=0)
    grad_got = swap_core(lax.dynamic_slice_in_dim(grad_part, (1 - c) * per_core, per_core, axis=0))
    grad_w_in = jnp.concatenate(
        [jnp.where(c == 0, grad_mine, grad_got), jnp.where(c == 0, grad_got, grad_mine)], axis=1
    ).T
    h_mine = acc[per_chip:].reshape(packed_rows, stack, 128).transpose(1, 0, 2)
    h_mine = h_mine.reshape(lanes, per_core, 128).transpose(1, 0, 2).reshape(per_core, regions)
    grad_w_out = jnp.dot(
        h_mine, g_region.astype(f32), precision=lax.Precision.HIGHEST, preferred_element_type=f32
    )

    dnorm = jnp.dot(g_in, w_in.T, preferred_element_type=f32).reshape(height, breadth, width)
    dconv = inv_std * (
        dnorm
        - jnp.mean(dnorm, axis=-1, keepdims=True)
        - normed_f * jnp.mean(dnorm * normed_f, axis=-1, keepdims=True)
    )
    dpad = widen(dconv.astype(bf16), c).astype(f32)
    dpad = lax.dynamic_update_slice(dpad, dconv, (3, 3, 0))
    back = depthwise(dpad, taps, height, breadth, True)
    kernel_rows = []
    for a in range(7):
        for b in range(7):
            kernel_rows.append(jnp.sum(xpad[a : a + height, b : b + breadth] * dconv, axis=(0, 1)))
    kernel_rows.append(jnp.zeros((width,), f32))
    parts = jnp.stack(kernel_rows, axis=0).reshape(2, 25, width)
    part = jnp.take(parts, c, axis=0) + swap_core(jnp.take(parts, 1 - c, axis=0))
    for bit in order_chip:
        part = part + exchange(part, (1 << bit, 1 << bit))
    part_other = swap_core(part)
    grad_kernel = jnp.concatenate(
        [jnp.where(c == 0, part, part_other), jnp.where(c == 0, part_other, part)], axis=0
    )[:49]
    grad_image = (dblock + back).astype(bf16)
    return (region_pool, grad_image, grad_w_in, grad_w_out, grad_kernel)


def solution(mesh):
    placed = (
        P(("slides", "row"), "col", None),
        P(),
        P(),
        P(),
        P(),
        P(("slides", "row"), "col"),
        P("slides"),
        P(("slides", "row", "col"), None),
    )
    return jax.shard_map(
        shards,
        mesh=mesh,
        in_specs=placed,
        out_specs=(
            P(("slides", "row", "col"), None),
            P(("slides", "row"), "col", None),
            P("slides", ("row", "col")),
            P(("slides", "row", "col"), None),
            P("slides", None),
        ),
        check_vma=False,
    )
```

```python
import functools
import math

import jax
import jax.numpy as jnp
from jax import lax
from jax.experimental import pallas as pl
from jax.experimental.pallas import tpu as pltpu
from jax.sharding import PartitionSpec as P


AXES = ("row", "col")
F32, BF16 = jnp.float32, jnp.bfloat16
VMEM = pl.BlockSpec(memory_space=pltpu.VMEM)
CONTRACT_ROWS = (((0,), (0,)), ((), ()))
CONTRACT_LANES = (((1,), (1,)), ((), ()))
LEFT = 8


def dot(a, b, dims=(((1,), (0,)), ((), ()))):
    return lax.dot_general(a, b, dims, preferred_element_type=F32)


def iota(shape, dim):
    return lax.broadcasted_iota(jnp.int32, shape, dim)


def call(body, outs, micros, scratch=(), far_in=(), any_in=(), far_out=(), room=8):
    def run(*operands):
        operands = [
            pltpu.with_memory_space_constraint(
                x, pltpu.HBM if k in far_in or k in any_in else pltpu.VMEM
            )
            for k, x in enumerate(operands)
        ]
        specs = [
            pl.BlockSpec(memory_space=pl.ANY) if k in any_in else VMEM
            for k in range(len(operands))
        ]
        shapes = [
            jax.ShapeDtypeStruct(shape, dtype) if k in far_out else pltpu.VMEM(shape, dtype)
            for k, (shape, dtype) in enumerate(outs)
        ]
        return pl.pallas_call(
            body,
            in_specs=specs,
            out_specs=[VMEM] * len(outs),
            out_shape=shapes,
            scratch_shapes=list(scratch),
            compiler_params=pltpu.CompilerParams(vmem_limit_bytes=room << 20),
            cost_estimate=pl.CostEstimate(
                flops=0, bytes_accessed=int(micros * 3.0e6), transcendentals=0
            ),
        )(*operands)

    return run


def exchange(value, chips, flip_core=False):
    rows = lax.axis_size("row")
    pairs = []
    for r in range(rows):
        for c in range(2):
            pairs.append((2 * r + c, 2 * (r ^ chips[c]) + (c ^ int(flip_core))))
    return lax.ppermute(value, AXES, pairs)


def swap_core(value):
    return exchange(value, (0, 0), True)


def swap_rows(value):
    rows = lax.axis_size("row")
    pairs = []
    for r in range(rows - 1):
        pairs.append((2 * r + 1, 2 * r + 2))
        pairs.append((2 * r + 2, 2 * r + 1))
    return lax.ppermute(value, AXES, pairs)


def orders(bits, chunk):
    plain = list(range(bits))
    mixed = [k ^ 1 if k < 2 and bits > 1 else k for k in range(bits)]
    turn = chunk * (bits // 2)
    return plain[turn:] + plain[:turn], mixed[turn:] + mixed[:turn]


def layout_place(chip, row, core, order):
    value = chip ^ row
    bits = len(order[0])
    out = jnp.zeros_like(value)
    for k in range(bits):
        taken = jnp.where(core == 0, (value >> order[0][k]) & 1, (value >> order[1][k]) & 1)
        out = out | (taken << (bits - 1 - k))
    return out


def prepare_body(
    ids_ref, table_ref, grad_ref, image_ref, taps_ref, scale_ref,
    known_ref, slot_ref, image_out, taps_out, scale_out, sems,
):
    copies = [
        pltpu.make_async_copy(image_ref, image_out, sems.at[0]),
        pltpu.make_async_copy(taps_ref, taps_out, sems.at[1]),
    ]
    for copy in copies:
        copy.start()
    scale_out[...] = scale_ref[...].reshape(scale_out.shape)
    tall, wide = ids_ref.shape
    regions = table_ref.shape[1]
    tiles = tall * wide
    owned = grad_ref.shape[0]
    eye = iota((wide, wide), 0) == iota((wide, wide), 1)
    columns = []
    for t in range(tall):
        row = jnp.broadcast_to(ids_ref[t : t + 1, :].astype(F32), (wide, wide))
        columns.append(jnp.sum(jnp.where(eye, row, 0.0), axis=1, keepdims=True))
    ids = jnp.concatenate(columns, axis=0)
    match = ids == iota((tiles, regions), 1).astype(F32)
    table = jnp.broadcast_to(table_ref[...].astype(F32), (tiles, regions))
    slot = jnp.sum(jnp.where(match, table, 0.0), axis=1, keepdims=True)
    onehot = (slot == iota((tiles, regions), 1).astype(F32)).astype(F32)
    known_ref[...] = jnp.zeros_like(known_ref)
    known_ref[:owned, :] = grad_ref[...]
    known_ref[owned : owned + 1, :regions] = jnp.sum(onehot, axis=0, keepdims=True).astype(BF16)
    places = tiles * 4
    p = iota((places, tiles), 0)
    line = 2 * wide
    tile = (p // (2 * line)) * wide + (p % line) // 2
    expand = (tile == iota((places, tiles), 1)).astype(F32)
    slot_row = jnp.sum(
        jnp.where(iota((tiles, tiles), 0) == iota((tiles, tiles), 1), slot, 0.0),
        axis=0,
        keepdims=True,
    )
    slot_ref[...] = jnp.sum(expand * slot_row, axis=1, keepdims=True)
    for copy in copies:
        copy.wait()


def prepare(ids, table, grad, image, taps, scale):
    width = grad.shape[1]
    outs = [
        ((8, width), BF16),
        ((4 * ids.size, 1), F32),
        (image.shape, BF16),
        (taps.shape, F32),
        ((1, width), F32),
    ]
    scratch = [pltpu.SemaphoreType.DMA((2,))]
    return call(
        prepare_body, outs, 1.5, scratch, far_in=(0, 1, 2, 5), any_in=(3, 4)
    )(ids, table.reshape(1, -1), grad, image, taps, scale)


def pack_body(own_ref, other_ref, out_ref):
    c = lax.axis_index("col")
    height, breadth, _ = own_ref.shape

    @pl.when(c == 0)
    def _():
        out_ref[:, :breadth] = own_ref[:3]
        out_ref[:, breadth:] = other_ref[:3]

    @pl.when(c == 1)
    def _():
        out_ref[:, :breadth] = other_ref[height - 3 :]
        out_ref[:, breadth:] = own_ref[height - 3 :]


def halo(source, field):
    _, breadth, width = field.shape
    other = swap_core(source)
    (packed,) = call(pack_body, [((3, 2 * breadth, width), field.dtype)], 0.5)(field, other)
    near = swap_rows(packed)
    far = swap_core(near)
    return other, near, far


def fill_center(pad_ref, own_ref, other_ref):
    c = lax.axis_index("col")
    height, breadth, lanes = other_ref.shape
    stop = LEFT + breadth
    for i in range(height):
        if len(own_ref.shape) == 3:
            own = own_ref[i]
        else:
            own = own_ref[i * breadth : (i + 1) * breadth, :]
        pad_ref[i, LEFT:stop, :] = own.astype(F32)

    @pl.when(c == 0)
    def _():
        pad_ref[:, stop : stop + 8, :] = other_ref[:, :8, :].astype(F32)
        pad_ref[:, :LEFT, :] = jnp.zeros((height, LEFT, lanes), F32)

    @pl.when(c == 1)
    def _():
        pad_ref[:, :LEFT, :] = other_ref[:, breadth - 8 :, :].astype(F32)
        pad_ref[:, stop : stop + 8, :] = jnp.zeros((height, 8, lanes), F32)


def fill_edges(edge_ref, near_ref, far_ref):
    c = lax.axis_index("col")
    breadth, lanes = near_ref.shape[1] // 2, near_ref.shape[2]
    stop = LEFT + breadth

    @pl.when(c == 0)
    def _():
        edge_ref[:3, LEFT : stop + 8, :] = near_ref[:, : breadth + 8, :].astype(F32)
        edge_ref[3:, LEFT : stop + 8, :] = far_ref[:, : breadth + 8, :].astype(F32)
        edge_ref[:, :LEFT, :] = jnp.zeros((6, LEFT, lanes), F32)

    @pl.when(c == 1)
    def _():
        edge_ref[:3, :stop, :] = far_ref[:, breadth - 8 :, :].astype(F32)
        edge_ref[3:, :stop, :] = near_ref[:, breadth - 8 :, :].astype(F32)
        edge_ref[:, stop : stop + 8, :] = jnp.zeros((6, 8, lanes), F32)


def convolve(lines, sums, taps_ref, breadth, lanes, flipped):
    sums = list(sums)
    height = len(sums)
    for b in range(7):
        start = LEFT - 3 + b
        for ref, at, i in lines:
            line = ref[at, start : start + breadth, lanes]
            for a in range(7):
                row = i - a
                if 0 <= row < height:
                    tap = 48 - (7 * a + b) if flipped else 7 * a + b
                    term = line * taps_ref[tap : tap + 1, lanes]
                    sums[row] = term if sums[row] is None else sums[row] + term
    return sums


def center_lines(ref):
    return [(ref, i, i + 3) for i in range(ref.shape[0])]


def edge_lines(ref, height):
    return [(ref, i, i) for i in range(3)] + [(ref, i + 3, i + height + 3) for i in range(3)]


def lane_block(k):
    return pl.ds(pl.multiple_of(k * 128, 128), 128)


def local_body(flipped, copied, *refs):
    own_ref, other_ref, taps_ref = refs[:3]
    sources = refs[3 : 3 + copied]
    pad_ref, sum_ref = refs[3 + copied : 5 + copied]
    targets = refs[5 + copied : 5 + 2 * copied]
    copies = []
    for k in range(copied):
        copies.append(pltpu.make_async_copy(sources[k], targets[k], refs[-1].at[k]))
        copies[k].start()
    height, breadth, width = other_ref.shape
    fill_center(pad_ref, own_ref, other_ref)

    def block(k, carry):
        lanes = lane_block(k)
        sums = convolve(
            center_lines(pad_ref), [None] * height, taps_ref, breadth, lanes, flipped
        )
        for i, row in enumerate(sums):
            sum_ref[i * breadth : (i + 1) * breadth, lanes] = row
        return carry

    lax.fori_loop(0, width // 128, block, 0)
    for copy in copies:
        copy.wait()


def local_convolution(own, other, taps, flipped=False, copied=()):
    height, breadth, width = other.shape
    outs = [((height, breadth + 16, width), F32), ((height * breadth, width), F32)]
    outs += [(x.shape, x.dtype) for x in copied]
    scratch = [pltpu.SemaphoreType.DMA((len(copied),))] if copied else []
    return call(
        functools.partial(local_body, flipped, len(copied)),
        outs,
        4.0,
        scratch,
        any_in=tuple(range(3, 3 + len(copied))),
    )(own, other, taps, *copied)


def conv_norm_body(
    near_ref, far_ref, taps_ref, sum_ref, edge_ref, normed_ref, send_ref, full_ref, inv_ref
):
    places, width = sum_ref.shape
    breadth = near_ref.shape[1] // 2
    height = places // breadth
    steps, half = width // 128, width // 2
    fill_edges(edge_ref, near_ref, far_ref)

    def block(k, carry):
        lanes = lane_block(k)
        sums = [sum_ref[i * breadth : (i + 1) * breadth, lanes] for i in range(height)]
        sums = convolve(edge_lines(edge_ref, height), sums, taps_ref, breadth, lanes, False)
        for i, row in enumerate(sums):
            full_ref[i * breadth : (i + 1) * breadth, lanes] = row
        return carry

    lax.fori_loop(0, steps, block, 0)

    def chunk(i, carry):
        rows = pl.ds(pl.multiple_of(i * 16, 16), 16)
        parts = [full_ref[rows, s * 128 : (s + 1) * 128] for s in range(steps)]
        mean = jnp.sum(functools.reduce(jnp.add, parts), axis=1, keepdims=True) * (1.0 / width)
        parts = [p - mean for p in parts]
        total = functools.reduce(jnp.add, [p * p for p in parts])
        var = jnp.sum(total, axis=1, keepdims=True) * (1.0 / width)
        inv = lax.rsqrt(var + 1e-06)
        inv_ref[rows, :] = jnp.broadcast_to(inv, (16, 128))
        for s, p in enumerate(parts):
            value = p * inv
            full_ref[rows, s * 128 : (s + 1) * 128] = value
            normed_ref[rows, s * 128 : (s + 1) * 128] = value.astype(BF16)
        return carry

    lax.fori_loop(0, places // 16, chunk, 0, unroll=4)
    c = lax.axis_index("col")
    send_ref[...] = normed_ref[:, pl.ds(pl.multiple_of((1 - c) * half, 128), half)]


def conv_norm(near, far, taps, sums):
    places, width = sums.shape
    outs = [
        ((6, near.shape[1] // 2 + 16, width), F32),
        ((places, width), BF16),
        ((places, width // 2), BF16),
        ((places, width), F32),
        ((places, 128), F32),
    ]
    return call(conv_norm_body, outs, 5.0)(near, far, taps, sums)


def lane_pack(rows, stack):
    _, wide = rows.shape
    tall = jnp.concatenate([rows[:, s : s + 128] for s in range(0, wide, 128)], axis=0)
    each = tall.shape[0] // stack
    return jnp.concatenate([tall[s * each : (s + 1) * each] for s in range(stack)], axis=1)


def lane_unpack(packed, n):
    _, wide = packed.shape
    tall = jnp.concatenate([packed[:, s : s + 128] for s in range(0, wide, 128)], axis=0)
    count = tall.shape[0] // n
    return jnp.concatenate([tall[s * n : (s + 1) * n] for s in range(count)], axis=1)


UNITS = 768


def unit_block(f):
    return pl.ds(pl.multiple_of(f * UNITS, UNITS), UNITS)


def forward_body(
    rows, normed_ref, w_in_ref, w_out_ref, slot_ref, image_ref, scale_ref,
    slope_ref, h_mine_ref, h_send_ref, s_mine_ref, s_send_ref, pre, hidden, branch, block,
):
    c = lax.axis_index("col")
    places, width = branch.shape
    total = w_in_ref.shape[1]
    regions = s_mine_ref.shape[0]
    half = width // 2
    per_chip = total // rows
    per_core = per_chip // 2
    slot = slot_ref[...]
    select = (slot == iota((places, regions), 1).astype(F32)).astype(BF16)
    branch[...] = jnp.zeros_like(branch)

    def units(f, carry):
        at = unit_block(f)
        pre[...] = dot(normed_ref[...], w_in_ref[:, at])

        def chunk(i, inner):
            line = pl.ds(pl.multiple_of(i * 16, 16), 16)
            for start in range(0, UNITS, 256):
                lanes = slice(start, start + 256)
                value = pre[line, lanes]
                cdf = 0.5 * (1.0 + lax.erf(value * (1.0 / math.sqrt(2.0))))
                density = jnp.exp(-0.5 * value * value) * (1.0 / math.sqrt(2.0 * math.pi))
                hidden[line, lanes] = (value * cdf).astype(BF16)
                out = pl.ds(pl.multiple_of(f * UNITS + start, 256), 256)
                slope_ref[line, out] = cdf + value * density
            return inner

        lax.fori_loop(0, places // 16, chunk, 0)
        branch[...] += dot(hidden[...], w_out_ref[at, :])
        by_region = dot(hidden[...], select, CONTRACT_ROWS)
        for t in range(UNITS // per_chip):
            q = f * (UNITS // per_chip) + t
            low = by_region[t * per_chip : t * per_chip + per_core]
            high = by_region[t * per_chip + per_core : (t + 1) * per_chip]
            h_mine_ref[q] = lane_pack(jnp.where(c == 0, low, high), half // 128)
            h_send_ref[q] = lane_pack(jnp.where(c == 0, high, low), half // 128).astype(BF16)
        return carry

    lax.fori_loop(0, total // UNITS, units, 0)
    block[...] = (image_ref[...].astype(F32) + scale_ref[...] * branch[...]).astype(BF16)
    for at, out in ((c, s_mine_ref), (1 - c, s_send_ref)):
        columns = block[:, pl.ds(pl.multiple_of(at * half, 128), half)]
        out[...] = dot(select, columns, CONTRACT_ROWS)


def mlp_forward(normed, w_in, w_out, slot, image, scale, regions, rows):
    places, width = normed.shape
    total, half = w_in.shape[1], width // 2
    packed = total // rows // 2 * regions // half
    outs = [
        ((places, total), F32),
        ((rows, packed, half), F32),
        ((rows, packed, half), BF16),
        ((regions, half), F32),
        ((regions, half), F32),
    ]
    scratch = [
        pltpu.VMEM((places, UNITS), F32),
        pltpu.VMEM((places, UNITS), BF16),
        pltpu.VMEM((places, width), F32),
        pltpu.VMEM((places, width), BF16),
    ]
    return call(functools.partial(forward_body, rows), outs, 9.0, scratch, room=12)(
        normed, w_in, w_out, slot, image, scale
    )


def backward_body(
    *refs,
):
    known_refs = refs[:4]
    slot_ref, scale_ref, w_out_ref, slope_ref = refs[4:8]
    g_in_ref, region_ref, dblock_ref, count_ref, g_out, known_all = refs[8:]
    r, c = lax.axis_index("row"), lax.axis_index("col")
    me = 2 * r + c
    places, units = slope_ref.shape
    regions = region_ref.shape[0]
    piece = known_refs[0].shape[0]
    for k in range(4):
        known_all[k * piece : (k + 1) * piece, :] = known_refs[k][...]
    total = 4 * piece
    owned = regions * 8 // total
    known = known_all[...]
    is_count = (iota((total, 128), 0) & 7) == owned
    count = dot(known[:, :regions], is_count.astype(BF16), CONTRACT_ROWS)
    count_ref[...] = count
    line = iota((regions, total), 1)
    source = (me ^ (line >> 3)) * owned + (line & 7)
    place = ((line & 7) < owned) & (source == iota((regions, total), 0))
    pooled = dot(place.astype(BF16), known)
    region_grad = (pooled / (4.0 * count[:, :1])).astype(BF16)
    g_region = (region_grad.astype(F32) * scale_ref[...]).astype(BF16)
    region_ref[...] = g_region
    select = (slot_ref[...] == iota((places, regions), 1).astype(F32)).astype(BF16)
    g_out[...] = dot(select, g_region).astype(BF16)
    dblock_ref[...] = dot(select, region_grad).astype(BF16)

    def block(f, carry):
        at = unit_block(f)
        dhidden = dot(g_out[...], w_out_ref[at, :], CONTRACT_LANES)
        g_in_ref[:, at] = (dhidden * slope_ref[:, at]).astype(BF16)
        return carry

    lax.fori_loop(0, units // UNITS, block, 0)


def mlp_backward(known, slot, scale, w_out, slope, regions):
    places, total = slope.shape
    width = w_out.shape[1]
    outs = [
        ((places, total), BF16),
        ((regions, width), BF16),
        ((places, width), BF16),
        ((regions, 128), F32),
    ]
    scratch = [
        pltpu.VMEM((places, width), BF16),
        pltpu.VMEM((4 * known[0].shape[0], width), BF16),
    ]
    return call(backward_body, outs, 4.0, scratch)(*known, slot, scale, w_out, slope)


def norm_backward_body(g_in_ref, w_in_ref, full_ref, inv_ref, dconv_ref, narrow_ref):
    places, width = dconv_ref.shape
    dconv_ref[...] = dot(g_in_ref[:, :UNITS], w_in_ref[:, :UNITS], CONTRACT_LANES)

    def block(f, carry):
        at = unit_block(f)
        dconv_ref[...] += dot(g_in_ref[:, at], w_in_ref[:, at], CONTRACT_LANES)
        return carry

    lax.fori_loop(1, w_in_ref.shape[1] // UNITS, block, 0)

    def chunk(i, carry):
        rows = pl.ds(pl.multiple_of(i * 16, 16), 16)
        lanes = [slice(s, s + 128) for s in range(0, width, 128)]
        grads = [dconv_ref[rows, at] for at in lanes]
        fulls = [full_ref[rows, at] for at in lanes]
        mean = jnp.sum(functools.reduce(jnp.add, grads), axis=1, keepdims=True) * (1.0 / width)
        total = functools.reduce(jnp.add, [g * n for g, n in zip(grads, fulls)])
        along = jnp.sum(total, axis=1, keepdims=True) * (1.0 / width)
        inv = inv_ref[rows, :]
        for at, g, n in zip(lanes, grads, fulls):
            value = inv * (g - mean - n * along)
            dconv_ref[rows, at] = value
            narrow_ref[rows, at] = value.astype(BF16)
        return carry

    lax.fori_loop(0, places // 16, chunk, 0, unroll=4)


def norm_backward(g_in, w_in, full, inv):
    places, width = full.shape
    outs = [((places, width), F32), ((places, width), BF16)]
    return call(norm_backward_body, outs, 4.0)(g_in, w_in, full, inv)


def split_high_low(value):
    high = value.astype(BF16)
    return high, (value - high.astype(F32)).astype(BF16)


CHUNKS = ((0, 256), (256, 128))


def weight_body(
    rows, own_ref, other_ref, normed_ref, normed_other_ref, h_mine_ref, h_got_ref, s_mine_ref,
    s_got_ref, *out_refs,
):
    r, c = lax.axis_index("row"), lax.axis_index("col")
    bits = rows.bit_length() - 1
    half = h_mine_ref.shape[2]
    total = own_ref.shape[1]
    count = rows // 2
    per_chip = total // rows
    packed = h_mine_ref.shape[1]
    per = s_mine_ref.shape[0] // rows
    columns = pl.ds(pl.multiple_of(c * half, 128), half)

    def store(q, value, first, split):
        for k, (lane, wide) in enumerate(CHUNKS):
            keep_ref, send_ref = out_refs[2 * k : 2 * k + 2]
            j = layout_place(q, r, c, orders(bits, k))
            part = value[:, lane : lane + wide]

            @pl.when(j < count)
            def _():
                keep_ref[j, first : first + value.shape[0], :] = part

            @pl.when(j >= count)
            def _():
                if split:
                    tail = jnp.concatenate(split_high_low(part), axis=0)
                else:
                    tail = part.astype(BF16)
                send_ref[j - count, first : first + tail.shape[0], :] = tail

    def block(f, carry):
        at = unit_block(f)
        grad = dot(own_ref[:, at], normed_ref[:, columns], CONTRACT_ROWS)
        grad += dot(other_ref[:, at], normed_other_ref[...], CONTRACT_ROWS)
        for t in range(UNITS // per_chip):
            q = f * (UNITS // per_chip) + t
            store(q, grad[t * per_chip : (t + 1) * per_chip], 0, False)
        return carry

    lax.fori_loop(0, total // UNITS, block, 0)

    def chip(q, carry):
        store(q, h_mine_ref[q] + h_got_ref[q].astype(F32), per_chip, False)
        at = pl.ds(pl.multiple_of(q * per, per), per)
        store(q, s_mine_ref[at, :] + s_got_ref[at, :], per_chip + packed, True)
        return carry

    lax.fori_loop(0, rows, chip, 0)


def weight_gradient(g_in, g_other, normed, normed_other, h_mine, h_got, s_mine, s_got):
    total = g_in.shape[1]
    rows, packed, _ = h_mine.shape
    per = s_mine.shape[0] // rows
    height = total // rows + packed + per
    outs = []
    for _, wide in CHUNKS:
        outs.append(((rows // 2, height, wide), F32))
        outs.append(((rows // 2, height + per, wide), BF16))
    return call(functools.partial(weight_body, rows), outs, 5.0, room=12)(
        g_in, g_other, normed, normed_other, h_mine, h_got, s_mine, s_got
    )


def merged(keep, got, per):
    body = keep.shape[0] - per
    plain = keep[:body] + got[:body].astype(F32)
    sums = keep[body:] + (got[body : body + per].astype(F32) + got[body + per :].astype(F32))
    return plain, sums


def round_body(per, old_ref, got_ref, keep_ref, send_ref):
    left = keep_ref.shape[0]
    body = keep_ref.shape[1] - per

    def near(i, carry):
        plain, sums = merged(old_ref[i], got_ref[i], per)
        keep_ref[i, :body, :] = plain
        keep_ref[i, body:, :] = sums
        return carry

    def far(i, carry):
        plain, sums = merged(old_ref[i + left], got_ref[i + left], per)
        send_ref[i, :body, :] = plain.astype(BF16)
        send_ref[i, body:, :] = jnp.concatenate(split_high_low(sums), axis=0)
        return carry

    lax.fori_loop(0, left, far, 0)
    lax.fori_loop(0, left, near, 0)


def halving_round(keep, got, per):
    count, height, wide = keep.shape
    left = count // 2
    outs = [((left, height, wide), F32), ((left, height + per, wide), BF16)]
    return call(functools.partial(round_body, per), outs, 0.5)(keep, got)


def finish_body(per, *refs):
    parts = refs[: 2 * len(CHUNKS)]
    region_ref, count_ref, out_ref, mine_ref, send_ref = refs[2 * len(CHUNKS) :]
    r, c = lax.axis_index("row"), lax.axis_index("col")
    done = [merged(parts[2 * k][0], parts[2 * k + 1][0], per) for k in range(len(CHUNKS))]
    plain = jnp.concatenate([d[0] for d in done], axis=1)
    sums = jnp.concatenate([d[1] for d in done], axis=1)
    per_core = out_ref.shape[0]
    first, second = plain[:per_core], plain[per_core : 2 * per_core]
    high, low = split_high_low(lane_unpack(plain[2 * per_core :], per_core))
    out_ref[...] = dot(high, region_ref[...]) + dot(low, region_ref[...])
    mine_ref[:per_core, :] = jnp.where(c == 0, first, second)
    send_ref[:per_core, :] = jnp.where(c == 0, second, first)
    start = pl.multiple_of(r * per, per)
    pooled = sums / (4.0 * count_ref[pl.ds(start, per), :1])
    mine_ref[per_core:, :] = pooled
    send_ref[per_core:, :] = pooled


def finish(parts, region, count, per, per_core):
    width = region.shape[1]
    part = ((per_core + per, width // 2), F32)
    outs = [((per_core, width), F32), part, part]
    return call(functools.partial(finish_body, per), outs, 1.0, far_out=(0,))(*parts, region, count)


def place_body(mine_ref, got_ref, grad_ref, pool_ref):
    c = lax.axis_index("col")
    per_core, width = grad_ref.shape
    half = width // 2
    owned = pool_ref.shape[0]
    for core in range(2):

        @pl.when(c == core)
        def _():
            left, right = (mine_ref, got_ref) if core == 0 else (got_ref, mine_ref)
            grad_ref[:, :half] = left[:per_core, :]
            grad_ref[:, half:] = right[:per_core, :]
            rows = slice(per_core + core * owned, per_core + (core + 1) * owned)
            pool_ref[:, :half] = left[rows, :]
            pool_ref[:, half:] = right[rows, :]


def place_outputs(mine, got, per_core, owned):
    width = 2 * mine.shape[1]
    outs = [((per_core, width), F32), ((owned, width), F32)]
    return call(place_body, outs, 0.5, far_out=(0, 1))(mine, got)


def kernel_gradient_body(pad_ref, edge_ref, dconv_ref, mine_ref, send_ref):
    c = lax.axis_index("col")
    height, wide, width = pad_ref.shape
    breadth = wide - 16

    def block(k, carry):
        lanes = lane_block(k)
        sums = {}
        grads = [dconv_ref[i * breadth : (i + 1) * breadth, lanes] for i in range(height)]
        for b in range(7):
            start = LEFT - 3 + b
            for ref, at, i in center_lines(pad_ref) + edge_lines(edge_ref, height):
                line = ref[at, start : start + breadth, lanes]
                for a in range(7):
                    row = i - a
                    if 0 <= row < height:
                        term = (line * grads[row]).reshape(breadth // 8, 8, 128).sum(axis=0)
                        sums[a, b] = sums[a, b] + term if (a, b) in sums else term
            for a in range(7):
                sums[a, b] = jnp.sum(sums[a, b], axis=0, keepdims=True)

        def put(ref, first, last):
            ref[24:, lanes] = jnp.zeros((8, 128), F32)
            for a in range(first, last):
                for b in range(7):
                    at = (a - first) * 7 + b
                    ref[at : at + 1, lanes] = sums[a, b]

        @pl.when(c == 0)
        def _():
            put(mine_ref, 0, 4)
            put(send_ref, 4, 7)

        @pl.when(c == 1)
        def _():
            put(mine_ref, 4, 7)
            put(send_ref, 0, 4)

        return carry

    lax.fori_loop(0, width // 128, block, 0)


def kernel_gradient(padded, edges, dconv):
    width = dconv.shape[1]
    outs = [((32, width), F32)] * 2
    return call(kernel_gradient_body, outs, 5.0)(padded, edges, dconv)


def back_body(near_ref, far_ref, taps_ref, sum_ref, dblock_ref, out_ref, edge_ref):
    height, breadth, width = out_ref.shape
    fill_edges(edge_ref, near_ref, far_ref)

    def block(k, carry):
        lanes = lane_block(k)
        sums = [sum_ref[i * breadth : (i + 1) * breadth, lanes] for i in range(height)]
        sums = convolve(edge_lines(edge_ref, height), sums, taps_ref, breadth, lanes, True)
        for i, row in enumerate(sums):
            rows = slice(i * breadth, (i + 1) * breadth)
            out_ref[i, :, lanes] = (dblock_ref[rows, lanes].astype(F32) + row).astype(BF16)
        return carry

    lax.fori_loop(0, width // 128, block, 0)


def back_convolution(near, far, taps, sums, dblock):
    places, width = sums.shape
    breadth = near.shape[1] // 2
    outs = [((places // breadth, breadth, width), BF16)]
    scratch = [pltpu.VMEM((6, breadth + 16, width), F32)]
    (out,) = call(back_body, outs, 3.0, scratch, far_out=(0,))(near, far, taps, sums, dblock)
    return out


def gather_known(known):
    bits = lax.axis_size("row").bit_length() - 1
    pieces = [known, swap_core(known)]
    for low in range(0, bits, 2):
        known = jnp.concatenate(pieces, axis=0)
        pieces = [known]
        for mask in (1 << low, 2 << low, 3 << low):
            pieces.append(exchange(known, (mask, mask)))
    return pieces


def compute(image, dw_kernel, w_in, w_out, layer_scale, region_ids, region_slot, pool_grad):
    height, breadth, width = image.shape
    total = w_in.shape[1]
    rows = lax.axis_size("row")
    bits = rows.bit_length() - 1
    c = lax.axis_index("col")
    regions = region_slot.shape[0]
    owned = pool_grad.shape[0]
    known, slot, own, taps, scale = prepare(
        region_ids, region_slot, pool_grad, image, dw_kernel, layer_scale
    )
    other, near, far = halo(image, own)
    known = gather_known(known)

    padded, sums, w_in, w_out = local_convolution(own, other, taps, copied=(w_in, w_out))
    edges, normed, normed_send, full, inv = conv_norm(near, far, taps, sums)
    normed_other = swap_core(normed_send)
    slope, h_mine, h_send, s_mine, s_send = mlp_forward(
        normed, w_in, w_out, slot, own.reshape(-1, width), scale, regions, rows
    )
    h_got = swap_core(h_send)
    s_got = swap_core(s_send)
    g_in, g_region, dblock, count = mlp_backward(known, slot, scale, w_out, slope, regions)
    g_other = swap_core(g_in)
    dconv, narrow = norm_backward(g_in, w_in, full, inv)
    halves = weight_gradient(g_in, g_other, normed, normed_other, h_mine, h_got, s_mine, s_got)
    per = regions // rows
    parts = []
    for k in range(len(CHUNKS)):
        keep, send = halves[2 * k : 2 * k + 2]
        order = orders(bits, k)
        for step in range(bits):
            got = exchange(send, (1 << order[0][step], 1 << order[1][step]))
            if step < bits - 1:
                keep, send = halving_round(keep, got, per)
        parts += [keep, got]

    part, part_send = kernel_gradient(padded, edges, dconv)
    part = part + swap_core(part_send)
    order = orders(bits, 1)
    for step in range(bits):
        part = part + exchange(part, (1 << order[0][step], 1 << order[1][step]))
    part_other = swap_core(part)
    grad_kernel = jnp.concatenate(
        [
            jnp.where(c == 0, part, part_other)[:28],
            jnp.where(c == 0, part_other, part)[:21],
        ],
        axis=0,
    )

    narrow = narrow.reshape(height, breadth, width)
    d_other, d_near, d_far = halo(narrow, narrow)
    _, back = local_convolution(dconv, d_other, taps, flipped=True)
    grad_image = back_convolution(d_near, d_far, taps, back, dblock)

    per_core = total // rows // 2
    grad_w_out, mine, send = finish(parts, g_region, count, per, per_core)
    got = swap_core(send)
    grad_w_in, region_pool = place_outputs(mine, got, per_core, owned)
    return (region_pool, grad_image, grad_w_in.T, grad_w_out, grad_kernel)


def solution(mesh):
    placed = (
        P(("slides", "row"), "col", None),
        P(),
        P(),
        P(),
        P(),
        P(("slides", "row"), "col"),
        P("slides"),
        P(("slides", "row", "col"), None),
    )
    return jax.shard_map(
        compute,
        mesh=mesh,
        in_specs=placed,
        out_specs=(
            P(("slides", "row", "col"), None),
            P(("slides", "row"), "col", None),
            P("slides", ("row", "col")),
            P(("slides", "row", "col"), None),
            P("slides", None),
        ),
        check_vma=False,
    )
```

```python
import functools
import math

import jax
import jax.numpy as jnp
from jax import lax
from jax.experimental import pallas as pl
from jax.experimental.pallas import tpu as pltpu
from jax.sharding import PartitionSpec as P


AXES = ("row", "col")
F32, BF16 = jnp.float32, jnp.bfloat16
VMEM = pl.BlockSpec(memory_space=pltpu.VMEM)
CONTRACT_ROWS = (((0,), (0,)), ((), ()))
CONTRACT_LANES = (((1,), (1,)), ((), ()))
LEFT = 8


def dot(a, b, dims=(((1,), (0,)), ((), ()))):
    return lax.dot_general(a, b, dims, preferred_element_type=F32)


def iota(shape, dim):
    return lax.broadcasted_iota(jnp.int32, shape, dim)


def call(body, outs, micros, scratch=(), far_in=(), any_in=(), far_out=(), room=8):
    def run(*operands):
        operands = [
            pltpu.with_memory_space_constraint(
                x, pltpu.HBM if k in far_in or k in any_in else pltpu.VMEM
            )
            for k, x in enumerate(operands)
        ]
        specs = [
            pl.BlockSpec(memory_space=pl.ANY) if k in any_in else VMEM
            for k in range(len(operands))
        ]
        shapes = [
            jax.ShapeDtypeStruct(shape, dtype) if k in far_out else pltpu.VMEM(shape, dtype)
            for k, (shape, dtype) in enumerate(outs)
        ]
        return pl.pallas_call(
            body,
            in_specs=specs,
            out_specs=[VMEM] * len(outs),
            out_shape=shapes,
            scratch_shapes=list(scratch),
            compiler_params=pltpu.CompilerParams(vmem_limit_bytes=room << 20),
            cost_estimate=pl.CostEstimate(
                flops=0, bytes_accessed=int(micros * 3.0e6), transcendentals=0
            ),
        )(*operands)

    return run


def exchange(value, chips, flip_core=False):
    rows = lax.axis_size("row")
    pairs = []
    for r in range(rows):
        for c in range(2):
            pairs.append((2 * r + c, 2 * (r ^ chips[c]) + (c ^ int(flip_core))))
    return lax.ppermute(value, AXES, pairs)


def swap_core(value):
    return exchange(value, (0, 0), True)


def swap_rows(value):
    rows = lax.axis_size("row")
    pairs = []
    for r in range(rows - 1):
        pairs.append((2 * r + 1, 2 * r + 2))
        pairs.append((2 * r + 2, 2 * r + 1))
    return lax.ppermute(value, AXES, pairs)


def orders(bits, chunk):
    plain = list(range(bits))
    if bits < 4:
        return plain, plain
    if chunk == 0:
        return [1, 2, 0] + plain[3:], [2, 1, 3, 0] + plain[4:]
    return plain, [0, 3, 1, 2] + plain[4:]


def layout_place(chip, row, core, order):
    value = chip ^ row
    bits = len(order[0])
    out = jnp.zeros_like(value)
    for k in range(bits):
        taken = jnp.where(core == 0, (value >> order[0][k]) & 1, (value >> order[1][k]) & 1)
        out = out | (taken << (bits - 1 - k))
    return out


def prepare_body(
    ids_ref, table_ref, grad_ref, image_ref, taps_ref, scale_ref,
    known_ref, slot_ref, image_out, taps_out, scale_out, sems,
):
    copies = [
        pltpu.make_async_copy(image_ref, image_out, sems.at[0]),
        pltpu.make_async_copy(taps_ref, taps_out, sems.at[1]),
    ]
    for copy in copies:
        copy.start()
    scale_out[...] = scale_ref[...].reshape(scale_out.shape)
    tall, wide = ids_ref.shape
    regions = table_ref.shape[1]
    tiles = tall * wide
    owned = grad_ref.shape[0]
    eye = iota((wide, wide), 0) == iota((wide, wide), 1)
    columns = []
    for t in range(tall):
        row = jnp.broadcast_to(ids_ref[t : t + 1, :].astype(F32), (wide, wide))
        columns.append(jnp.sum(jnp.where(eye, row, 0.0), axis=1, keepdims=True))
    ids = jnp.concatenate(columns, axis=0)
    match = ids == iota((tiles, regions), 1).astype(F32)
    table = jnp.broadcast_to(table_ref[...].astype(F32), (tiles, regions))
    slot = jnp.sum(jnp.where(match, table, 0.0), axis=1, keepdims=True)
    onehot = (slot == iota((tiles, regions), 1).astype(F32)).astype(F32)
    known_ref[...] = jnp.zeros_like(known_ref)
    known_ref[:owned, :] = grad_ref[...]
    known_ref[owned : owned + 1, :regions] = jnp.sum(onehot, axis=0, keepdims=True).astype(BF16)
    places = tiles * 4
    p = iota((places, tiles), 0)
    line = 2 * wide
    tile = (p // (2 * line)) * wide + (p % line) // 2
    expand = (tile == iota((places, tiles), 1)).astype(F32)
    slot_row = jnp.sum(
        jnp.where(iota((tiles, tiles), 0) == iota((tiles, tiles), 1), slot, 0.0),
        axis=0,
        keepdims=True,
    )
    slot_ref[...] = jnp.sum(expand * slot_row, axis=1, keepdims=True)
    for copy in copies:
        copy.wait()


def prepare(ids, table, grad, image, taps, scale):
    width = grad.shape[1]
    outs = [
        ((8, width), BF16),
        ((4 * ids.size, 1), F32),
        (image.shape, BF16),
        (taps.shape, F32),
        ((1, width), F32),
    ]
    scratch = [pltpu.SemaphoreType.DMA((2,))]
    return call(
        prepare_body, outs, 1.5, scratch, far_in=(0, 1, 2, 5), any_in=(3, 4)
    )(ids, table.reshape(1, -1), grad, image, taps, scale)


def pack_body(own_ref, other_ref, out_ref):
    c = lax.axis_index("col")
    height, breadth, _ = own_ref.shape

    @pl.when(c == 0)
    def _():
        out_ref[:, :breadth] = own_ref[:3]
        out_ref[:, breadth:] = other_ref[:3]

    @pl.when(c == 1)
    def _():
        out_ref[:, :breadth] = other_ref[height - 3 :]
        out_ref[:, breadth:] = own_ref[height - 3 :]


def halo(source, field):
    _, breadth, width = field.shape
    other = swap_core(source)
    (packed,) = call(pack_body, [((3, 2 * breadth, width), field.dtype)], 0.5)(field, other)
    near = swap_rows(packed)
    far = swap_core(near)
    return other, near, far


def fill_center(pad_ref, own_ref, other_ref):
    c = lax.axis_index("col")
    height, breadth, lanes = other_ref.shape
    stop = LEFT + breadth
    for i in range(height):
        if len(own_ref.shape) == 3:
            own = own_ref[i]
        else:
            own = own_ref[i * breadth : (i + 1) * breadth, :]
        pad_ref[i, LEFT:stop, :] = own.astype(F32)

    @pl.when(c == 0)
    def _():
        pad_ref[:, stop : stop + 8, :] = other_ref[:, :8, :].astype(F32)
        pad_ref[:, :LEFT, :] = jnp.zeros((height, LEFT, lanes), F32)

    @pl.when(c == 1)
    def _():
        pad_ref[:, :LEFT, :] = other_ref[:, breadth - 8 :, :].astype(F32)
        pad_ref[:, stop : stop + 8, :] = jnp.zeros((height, 8, lanes), F32)


def fill_edges(edge_ref, near_ref, far_ref):
    c = lax.axis_index("col")
    breadth, lanes = near_ref.shape[1] // 2, near_ref.shape[2]
    stop = LEFT + breadth

    @pl.when(c == 0)
    def _():
        edge_ref[:3, LEFT : stop + 8, :] = near_ref[:, : breadth + 8, :].astype(F32)
        edge_ref[3:, LEFT : stop + 8, :] = far_ref[:, : breadth + 8, :].astype(F32)
        edge_ref[:, :LEFT, :] = jnp.zeros((6, LEFT, lanes), F32)

    @pl.when(c == 1)
    def _():
        edge_ref[:3, :stop, :] = far_ref[:, breadth - 8 :, :].astype(F32)
        edge_ref[3:, :stop, :] = near_ref[:, breadth - 8 :, :].astype(F32)
        edge_ref[:, stop : stop + 8, :] = jnp.zeros((6, 8, lanes), F32)


def convolve(lines, sums, taps_ref, breadth, lanes, flipped):
    sums = list(sums)
    height = len(sums)
    for b in range(7):
        start = LEFT - 3 + b
        for ref, at, i in lines:
            line = ref[at, start : start + breadth, lanes]
            for a in range(7):
                row = i - a
                if 0 <= row < height:
                    tap = 48 - (7 * a + b) if flipped else 7 * a + b
                    term = line * taps_ref[tap : tap + 1, lanes]
                    sums[row] = term if sums[row] is None else sums[row] + term
    return sums


def center_lines(ref):
    return [(ref, i, i + 3) for i in range(ref.shape[0])]


def edge_lines(ref, height):
    return [(ref, i, i) for i in range(3)] + [(ref, i + 3, i + height + 3) for i in range(3)]


def over_lanes(width, block):
    def step(k, carry):
        for side in range(2):
            block(pl.ds(pl.multiple_of(k * 256 + side * 128, 128), 128))
        return carry

    lax.fori_loop(0, width // 256, step, 0)


def local_body(flipped, copied, *refs):
    own_ref, other_ref, taps_ref = refs[:3]
    sources = refs[3 : 3 + copied]
    pad_ref, sum_ref = refs[3 + copied : 5 + copied]
    targets = refs[5 + copied : 5 + 2 * copied]
    copies = []
    for k in range(copied):
        copies.append(pltpu.make_async_copy(sources[k], targets[k], refs[-1].at[k]))
        copies[k].start()
    height, breadth, width = other_ref.shape
    fill_center(pad_ref, own_ref, other_ref)

    def block(lanes):
        sums = convolve(
            center_lines(pad_ref), [None] * height, taps_ref, breadth, lanes, flipped
        )
        for i, row in enumerate(sums):
            sum_ref[i * breadth : (i + 1) * breadth, lanes] = row

    over_lanes(width, block)
    for copy in copies:
        copy.wait()


def local_convolution(own, other, taps, flipped=False, copied=()):
    height, breadth, width = other.shape
    outs = [((height, breadth + 16, width), F32), ((height * breadth, width), F32)]
    outs += [(x.shape, x.dtype) for x in copied]
    scratch = [pltpu.SemaphoreType.DMA((len(copied),))] if copied else []
    return call(
        functools.partial(local_body, flipped, len(copied)),
        outs,
        4.0,
        scratch,
        any_in=tuple(range(3, 3 + len(copied))),
    )(own, other, taps, *copied)


def conv_norm_body(
    near_ref, far_ref, taps_ref, sum_ref, edge_ref, normed_ref, send_ref, full_ref, inv_ref
):
    places, width = sum_ref.shape
    breadth = near_ref.shape[1] // 2
    height = places // breadth
    steps, half = width // 128, width // 2
    fill_edges(edge_ref, near_ref, far_ref)

    for k in range(0, width, 128):
        lanes = slice(k, k + 128)
        sums = [sum_ref[i * breadth : (i + 1) * breadth, lanes] for i in range(height)]
        sums = convolve(edge_lines(edge_ref, height), sums, taps_ref, breadth, lanes, False)
        for i, row in enumerate(sums):
            full_ref[i * breadth : (i + 1) * breadth, lanes] = row

    for i in range(0, places, 16):
        rows = slice(i, i + 16)
        parts = [full_ref[rows, s * 128 : (s + 1) * 128] for s in range(steps)]
        mean = jnp.sum(functools.reduce(jnp.add, parts), axis=1, keepdims=True) * (1.0 / width)
        parts = [p - mean for p in parts]
        total = functools.reduce(jnp.add, [p * p for p in parts])
        var = jnp.sum(total, axis=1, keepdims=True) * (1.0 / width)
        inv = lax.rsqrt(var + 1e-06)
        inv_ref[rows, :] = jnp.broadcast_to(inv, (16, 128))
        for s, p in enumerate(parts):
            value = p * inv
            full_ref[rows, s * 128 : (s + 1) * 128] = value
            normed_ref[rows, s * 128 : (s + 1) * 128] = value.astype(BF16)
    c = lax.axis_index("col")
    send_ref[...] = normed_ref[:, pl.ds(pl.multiple_of((1 - c) * half, 128), half)]


def conv_norm(near, far, taps, sums):
    places, width = sums.shape
    outs = [
        ((6, near.shape[1] // 2 + 16, width), F32),
        ((places, width), BF16),
        ((places, width // 2), BF16),
        ((places, width), F32),
        ((places, 128), F32),
    ]
    return call(conv_norm_body, outs, 5.0)(near, far, taps, sums)


def lane_pack(rows, stack):
    _, wide = rows.shape
    tall = jnp.concatenate([rows[:, s : s + 128] for s in range(0, wide, 128)], axis=0)
    each = tall.shape[0] // stack
    return jnp.concatenate([tall[s * each : (s + 1) * each] for s in range(stack)], axis=1)


def lane_unpack(packed, n):
    _, wide = packed.shape
    tall = jnp.concatenate([packed[:, s : s + 128] for s in range(0, wide, 128)], axis=0)
    count = tall.shape[0] // n
    return jnp.concatenate([tall[s * n : (s + 1) * n] for s in range(count)], axis=1)


UNITS = 768


def forward_body(
    rows, normed_ref, w_in_ref, w_out_ref, slot_ref, image_ref, scale_ref,
    slope_ref, h_mine_ref, h_send_ref, s_mine_ref, s_send_ref, pre, hidden, branch, block,
):
    c = lax.axis_index("col")
    places, width = branch.shape
    total = w_in_ref.shape[1]
    regions = s_mine_ref.shape[0]
    half = width // 2
    per_chip = total // rows
    per_core = per_chip // 2
    slot = slot_ref[...]
    select = (slot == iota((places, regions), 1).astype(F32)).astype(BF16)
    blocks = total // UNITS

    def expand(f):
        pre[f % 2] = dot(normed_ref[...], w_in_ref[:, f * UNITS : (f + 1) * UNITS])

    def activate(f):
        for row in range(0, places, 16):
            line = slice(row, row + 16)
            for start in range(0, UNITS, 256):
                value = pre[f % 2, line, start : start + 256]
                cdf = 0.5 * (1.0 + lax.erf(value * (1.0 / math.sqrt(2.0))))
                density = jnp.exp(-0.5 * value * value) * (1.0 / math.sqrt(2.0 * math.pi))
                hidden[f % 2, line, start : start + 256] = (value * cdf).astype(BF16)
                at = f * UNITS + start
                slope_ref[line, at : at + 256] = cdf + value * density

    def reduce(f):
        part = dot(hidden[f % 2], w_out_ref[f * UNITS : (f + 1) * UNITS, :])
        branch[...] = part if f == 0 else branch[...] + part
        by_region = dot(hidden[f % 2], select, CONTRACT_ROWS)
        for t in range(UNITS // per_chip):
            q = f * (UNITS // per_chip) + t
            low = by_region[t * per_chip : t * per_chip + per_core]
            high = by_region[t * per_chip + per_core : (t + 1) * per_chip]
            h_mine_ref[q] = lane_pack(jnp.where(c == 0, low, high), half // 128)
            h_send_ref[q] = lane_pack(jnp.where(c == 0, high, low), half // 128).astype(BF16)

    expand(0)
    for f in range(blocks):
        if f + 1 < blocks:
            expand(f + 1)
        activate(f)
        reduce(f)
    block[...] = (image_ref[...].astype(F32) + scale_ref[...] * branch[...]).astype(BF16)
    for at, out in ((c, s_mine_ref), (1 - c, s_send_ref)):
        columns = block[:, pl.ds(pl.multiple_of(at * half, 128), half)]
        out[...] = dot(select, columns, CONTRACT_ROWS)


def mlp_forward(normed, w_in, w_out, slot, image, scale, regions, rows):
    places, width = normed.shape
    total, half = w_in.shape[1], width // 2
    packed = total // rows // 2 * regions // half
    outs = [
        ((places, total), F32),
        ((rows, packed, half), F32),
        ((rows, packed, half), BF16),
        ((regions, half), F32),
        ((regions, half), F32),
    ]
    scratch = [
        pltpu.VMEM((2, places, UNITS), F32),
        pltpu.VMEM((2, places, UNITS), BF16),
        pltpu.VMEM((places, width), F32),
        pltpu.VMEM((places, width), BF16),
    ]
    return call(functools.partial(forward_body, rows), outs, 9.0, scratch, room=12)(
        normed, w_in, w_out, slot, image, scale
    )


def backward_body(
    *refs,
):
    known_refs = refs[:4]
    slot_ref, scale_ref, w_out_ref, slope_ref = refs[4:8]
    g_in_ref, region_ref, dblock_ref, count_ref, g_out, known_all = refs[8:]
    r, c = lax.axis_index("row"), lax.axis_index("col")
    me = 2 * r + c
    places, units = slope_ref.shape
    regions = region_ref.shape[0]
    piece = known_refs[0].shape[0]
    for k in range(4):
        known_all[k * piece : (k + 1) * piece, :] = known_refs[k][...]
    total = 4 * piece
    owned = regions * 8 // total
    known = known_all[...]
    is_count = (iota((total, 128), 0) & 7) == owned
    count = dot(known[:, :regions], is_count.astype(BF16), CONTRACT_ROWS)
    count_ref[...] = count
    line = iota((regions, total), 1)
    bits = (total >> 4).bit_length() - 1
    source = gathered_device(line >> 3, me, bits) * owned + (line & 7)
    place = ((line & 7) < owned) & (source == iota((regions, total), 0))
    pooled = dot(place.astype(BF16), known)
    region_grad = (pooled / (4.0 * count[:, :1])).astype(BF16)
    g_region = (region_grad.astype(F32) * scale_ref[...]).astype(BF16)
    region_ref[...] = g_region
    select = (slot_ref[...] == iota((places, regions), 1).astype(F32)).astype(BF16)
    g_out[...] = dot(select, g_region).astype(BF16)
    dblock_ref[...] = dot(select, region_grad).astype(BF16)

    for f in range(0, units, UNITS):
        at = slice(f, f + UNITS)
        dhidden = dot(g_out[...], w_out_ref[at, :], CONTRACT_LANES)
        g_in_ref[:, at] = (dhidden * slope_ref[:, at]).astype(BF16)


def mlp_backward(known, slot, scale, w_out, slope, regions):
    places, total = slope.shape
    width = w_out.shape[1]
    outs = [
        ((places, total), BF16),
        ((regions, width), BF16),
        ((places, width), BF16),
        ((regions, 128), F32),
    ]
    scratch = [
        pltpu.VMEM((places, width), BF16),
        pltpu.VMEM((4 * known[0].shape[0], width), BF16),
    ]
    return call(backward_body, outs, 4.0, scratch)(*known, slot, scale, w_out, slope)


def norm_backward_body(g_in_ref, w_in_ref, full_ref, inv_ref, dconv_ref, narrow_ref):
    places, width = dconv_ref.shape
    dconv_ref[...] = dot(g_in_ref[...], w_in_ref[...], CONTRACT_LANES)

    for i in range(0, places, 16):
        rows = slice(i, i + 16)
        lanes = [slice(s, s + 128) for s in range(0, width, 128)]
        grads = [dconv_ref[rows, at] for at in lanes]
        fulls = [full_ref[rows, at] for at in lanes]
        mean = jnp.sum(functools.reduce(jnp.add, grads), axis=1, keepdims=True) * (1.0 / width)
        total = functools.reduce(jnp.add, [g * n for g, n in zip(grads, fulls)])
        along = jnp.sum(total, axis=1, keepdims=True) * (1.0 / width)
        inv = inv_ref[rows, :]
        for at, g, n in zip(lanes, grads, fulls):
            value = inv * (g - mean - n * along)
            dconv_ref[rows, at] = value
            narrow_ref[rows, at] = value.astype(BF16)


def norm_backward(g_in, w_in, full, inv):
    places, width = full.shape
    outs = [((places, width), F32), ((places, width), BF16)]
    return call(norm_backward_body, outs, 4.0)(g_in, w_in, full, inv)


def split_high_low(value):
    high = value.astype(BF16)
    return high, (value - high.astype(F32)).astype(BF16)


CHUNKS = ((0, 256), (256, 128))


def weight_body(
    rows, own_ref, other_ref, normed_ref, normed_other_ref, h_mine_ref, h_got_ref, s_mine_ref,
    s_got_ref, *out_refs,
):
    r, c = lax.axis_index("row"), lax.axis_index("col")
    bits = rows.bit_length() - 1
    half = h_mine_ref.shape[2]
    total = own_ref.shape[1]
    count = rows // 2
    per_chip = total // rows
    packed = h_mine_ref.shape[1]
    per = s_mine_ref.shape[0] // rows
    columns = pl.ds(pl.multiple_of(c * half, 128), half)

    def store(q, value, first):
        for k, (lane, wide) in enumerate(CHUNKS):
            j = layout_place(jnp.int32(q), r, c, orders(bits, k))
            out_refs[2 * k][j, first : first + value.shape[0], :] = value[:, lane : lane + wide]

    for q in range(rows):
        store(q, h_mine_ref[q] + h_got_ref[q].astype(F32), per_chip)
        at = slice(q * per, (q + 1) * per)
        store(q, s_mine_ref[at, :] + s_got_ref[at, :], per_chip + packed)
    for f in range(0, total, UNITS):
        at = slice(f, f + UNITS)
        grad = dot(own_ref[:, at], normed_ref[:, columns], CONTRACT_ROWS)
        grad += dot(other_ref[:, at], normed_other_ref[...], CONTRACT_ROWS)
        for t in range(UNITS // per_chip):
            store((f + t * per_chip) // per_chip, grad[t * per_chip : (t + 1) * per_chip], 0)
    body = per_chip + packed
    for k in range(len(CHUNKS)):
        all_ref, send_ref = out_refs[2 * k : 2 * k + 2]
        for j in range(count):
            send_ref[j, :body, :] = all_ref[count + j, :body, :].astype(BF16)
            sums = all_ref[count + j, body:, :]
            send_ref[j, body:, :] = jnp.concatenate(split_high_low(sums), axis=0)


def weight_gradient(g_in, g_other, normed, normed_other, h_mine, h_got, s_mine, s_got):
    total = g_in.shape[1]
    rows, packed, _ = h_mine.shape
    per = s_mine.shape[0] // rows
    height = total // rows + packed + per
    outs = []
    for _, wide in CHUNKS:
        outs.append(((rows, height, wide), F32))
        outs.append(((rows // 2, height + per, wide), BF16))
    return call(functools.partial(weight_body, rows), outs, 5.0, room=12)(
        g_in, g_other, normed, normed_other, h_mine, h_got, s_mine, s_got
    )


def merged(keep, got, per):
    body = keep.shape[0] - per
    plain = keep[:body] + got[:body].astype(F32)
    sums = keep[body:] + (got[body : body + per].astype(F32) + got[body + per :].astype(F32))
    return plain, sums


def round_body(per, old_ref, got_ref, keep_ref, send_ref):
    left = keep_ref.shape[0]
    body = keep_ref.shape[1] - per

    def near(i, carry):
        plain, sums = merged(old_ref[i], got_ref[i], per)
        keep_ref[i, :body, :] = plain
        keep_ref[i, body:, :] = sums
        return carry

    def far(i, carry):
        plain, sums = merged(old_ref[i + left], got_ref[i + left], per)
        send_ref[i, :body, :] = plain.astype(BF16)
        send_ref[i, body:, :] = jnp.concatenate(split_high_low(sums), axis=0)
        return carry

    lax.fori_loop(0, left, far, 0)
    lax.fori_loop(0, left, near, 0)


def halving_round(keep, got, per):
    _, height, wide = keep.shape
    left = got.shape[0] // 2
    outs = [((left, height, wide), F32), ((left, height + per, wide), BF16)]
    return call(functools.partial(round_body, per), outs, 0.5)(keep, got)


def taps_to_rows(taps):
    return jnp.concatenate(
        [taps[:, k : k + 128] for k in range(0, taps.shape[1], 128)], axis=0
    )


def rows_to_taps(rows, count):
    pieces = [rows[k : k + count] for k in range(0, rows.shape[0], count)]
    return jnp.concatenate(pieces, axis=1)


def taps_received(got_ref, first, count):
    rows = (got_ref.shape[0] - first) // 2
    high = got_ref[first : first + rows, :].astype(F32)
    return rows_to_taps(high + got_ref[first + rows :, :].astype(F32), count)


def tapped_round_body(
    per, carried, old_ref, got_ref, taps_ref, taps_got_ref, keep_ref, send_ref, taps_out_ref
):
    left = keep_ref.shape[0]
    height = keep_ref.shape[1] + per
    body = keep_ref.shape[1] - per

    def block(i):
        at = pl.ds(pl.multiple_of(i * height, 16), height)
        return merged(old_ref[i], got_ref[at, :], per)

    def near(i, carry):
        plain, sums = block(i)
        keep_ref[i, :body, :] = plain
        keep_ref[i, body:, :] = sums
        return carry

    def far(i, carry):
        plain, sums = block(i + left)
        send_ref[pl.ds(pl.multiple_of(i * height, 16), body), :] = plain.astype(BF16)
        tail = pl.ds(pl.multiple_of(i * height + body, 16), 2 * per)
        send_ref[tail, :] = jnp.concatenate(split_high_low(sums), axis=0)
        return carry

    lax.fori_loop(0, left, far, 0)
    count = taps_ref.shape[0]
    if carried:
        taps = taps_ref[...] + taps_received(got_ref, 2 * left * height, count)
    else:
        taps = taps_ref[...] + taps_got_ref[...]
    high, low = split_high_low(taps)
    taps_out_ref[...] = high.astype(F32) + low.astype(F32)
    rows = taps_to_rows(taps).shape[0]
    high, low = split_high_low(taps_to_rows(taps))
    send_ref[left * height : left * height + rows, :] = high
    send_ref[left * height + rows :, :] = low
    lax.fori_loop(0, left, near, 0)


def tapped_round(keep, got, taps, taps_got, left, per):
    _, height, wide = keep.shape
    rows = taps.size // wide
    outs = [
        ((left, height, wide), F32),
        ((left * (height + per) + 2 * rows, wide), BF16),
        (taps.shape, F32),
    ]
    carried = taps_got is None
    body = functools.partial(tapped_round_body, per, carried)
    return call(body, outs, 0.5)(keep, got.reshape(-1, wide), taps, taps if carried else taps_got)


def finish_body(per, *refs):
    keep_a, got_a, keep_b, got_b, taps_ref, region_ref, count_ref = refs[:7]
    out_ref, mine_ref, send_ref = refs[7:]
    r, c = lax.axis_index("row"), lax.axis_index("col")
    height = keep_b.shape[1] + per
    done = [merged(keep_a[0], got_a[0], per), merged(keep_b[0], got_b[:height, :], per)]
    plain = jnp.concatenate([d[0] for d in done], axis=1)
    sums = jnp.concatenate([d[1] for d in done], axis=1)
    per_core = out_ref.shape[0]
    half = plain.shape[1]
    first, second = plain[:per_core], plain[per_core : 2 * per_core]
    high, low = split_high_low(lane_unpack(plain[2 * per_core :], per_core))
    out_ref[...] = dot(high, region_ref[...]) + dot(low, region_ref[...])
    mine_ref[:per_core, :] = jnp.where(c == 0, first, second)
    send_ref[:per_core, :] = jnp.where(c == 0, second, first)
    start = pl.multiple_of(r * per, per)
    pooled = sums / (4.0 * count_ref[pl.ds(start, per), :1])
    count = taps_ref.shape[0]
    taps = taps_ref[...] + taps_received(got_b, height, count)
    for ref in (mine_ref, send_ref):
        ref[per_core : per_core + per, :] = pooled
        ref[per_core + per : per_core + per + count, :] = taps[:, :half]
        ref[per_core + per + count :, :] = taps[:, half:]


def finish(parts, taps, region, count, per, per_core):
    width = region.shape[1]
    part = ((per_core + per + 2 * taps.shape[0], width // 2), F32)
    outs = [((per_core, width), F32), part, part]
    return call(functools.partial(finish_body, per), outs, 1.0, far_out=(0,))(
        *parts, taps, region, count
    )


def place_body(per, mine_ref, got_ref, grad_ref, pool_ref, taps_ref):
    c = lax.axis_index("col")
    per_core, width = grad_ref.shape
    half = width // 2
    owned = pool_ref.shape[0]
    first = per_core + per
    count = (mine_ref.shape[0] - first) // 2
    for core in range(2):

        @pl.when(c == core)
        def _():
            left, right = (mine_ref, got_ref) if core == 0 else (got_ref, mine_ref)
            grad_ref[:, :half] = left[:per_core, :]
            grad_ref[:, half:] = right[:per_core, :]
            rows = slice(per_core + core * owned, per_core + (core + 1) * owned)
            pool_ref[:, :half] = left[rows, :]
            pool_ref[:, half:] = right[rows, :]
            for k in range(2):
                at = slice(k * half, (k + 1) * half)
                low = first + k * count
                taps_ref[:28, at] = left[low : low + 28, :]
                taps_ref[28:, at] = right[low : low + 21, :]


def place_outputs(mine, got, per_core, owned, per):
    width = 2 * mine.shape[1]
    outs = [((per_core, width), F32), ((owned, width), F32), ((49, width), F32)]
    return call(functools.partial(place_body, per), outs, 0.5, far_out=(0, 1, 2))(mine, got)


def kernel_gradient_body(pad_ref, edge_ref, dconv_ref, mine_ref, send_ref):
    c = lax.axis_index("col")
    height, wide, width = pad_ref.shape
    breadth = wide - 16

    def block(lanes):
        sums = {}
        grads = [dconv_ref[i * breadth : (i + 1) * breadth, lanes] for i in range(height)]
        for b in range(7):
            start = LEFT - 3 + b
            for ref, at, i in center_lines(pad_ref) + edge_lines(edge_ref, height):
                line = ref[at, start : start + breadth, lanes]
                for a in range(7):
                    row = i - a
                    if 0 <= row < height:
                        term = (line * grads[row]).reshape(breadth // 8, 8, 128).sum(axis=0)
                        sums[a, b] = sums[a, b] + term if (a, b) in sums else term
            for a in range(7):
                sums[a, b] = jnp.sum(sums[a, b], axis=0, keepdims=True)

        def put(ref, first, last):
            ref[24:, lanes] = jnp.zeros((8, 128), F32)
            for a in range(first, last):
                for b in range(7):
                    at = (a - first) * 7 + b
                    ref[at : at + 1, lanes] = sums[a, b]

        @pl.when(c == 0)
        def _():
            put(mine_ref, 0, 4)
            put(send_ref, 4, 7)

        @pl.when(c == 1)
        def _():
            put(mine_ref, 4, 7)
            put(send_ref, 0, 4)

    over_lanes(width, block)


def kernel_gradient(padded, edges, dconv):
    width = dconv.shape[1]
    outs = [((32, width), F32)] * 2
    return call(kernel_gradient_body, outs, 5.0)(padded, edges, dconv)


def back_body(near_ref, far_ref, taps_ref, sum_ref, dblock_ref, out_ref, edge_ref):
    height, breadth, width = out_ref.shape
    fill_edges(edge_ref, near_ref, far_ref)

    def block(lanes):
        sums = [sum_ref[i * breadth : (i + 1) * breadth, lanes] for i in range(height)]
        sums = convolve(edge_lines(edge_ref, height), sums, taps_ref, breadth, lanes, True)
        for i, row in enumerate(sums):
            rows = slice(i * breadth, (i + 1) * breadth)
            out_ref[i, :, lanes] = (dblock_ref[rows, lanes].astype(F32) + row).astype(BF16)

    over_lanes(width, block)


def back_convolution(near, far, taps, sums, dblock):
    places, width = sums.shape
    breadth = near.shape[1] // 2
    outs = [((places // breadth, breadth, width), BF16)]
    scratch = [pltpu.VMEM((6, breadth + 16, width), F32)]
    (out,) = call(back_body, outs, 3.0, scratch, far_out=(0,))(near, far, taps, sums, dblock)
    return out


def gather_stages(bits):
    return list(range((bits - 1) // 2 * 2, -1, -2))


def gather_known(known):
    bits = lax.axis_size("row").bit_length() - 1
    pieces = [known, swap_core(known)]
    for low in gather_stages(bits):
        known = jnp.concatenate(pieces, axis=0)
        pieces = [known]
        for mask in (1 << low, 2 << low, 3 << low):
            pieces.append(exchange(known, (mask, mask)))
    return pieces


def gathered_device(block, me, bits):
    mask = block & 1
    for k, low in enumerate(gather_stages(bits)):
        mask = mask | (((block >> (2 * k + 1)) & 3) << (low + 1))
    return me ^ mask


def compute(image, dw_kernel, w_in, w_out, layer_scale, region_ids, region_slot, pool_grad):
    height, breadth, width = image.shape
    total = w_in.shape[1]
    rows = lax.axis_size("row")
    bits = rows.bit_length() - 1
    regions = region_slot.shape[0]
    owned = pool_grad.shape[0]
    known, slot, own, taps, scale = prepare(
        region_ids, region_slot, pool_grad, image, dw_kernel, layer_scale
    )
    other, near, far = halo(image, own)
    known = gather_known(known)

    padded, sums, w_in, w_out = local_convolution(own, other, taps, copied=(w_in, w_out))
    edges, normed, normed_send, full, inv = conv_norm(near, far, taps, sums)
    normed_other = swap_core(normed_send)
    slope, h_mine, h_send, s_mine, s_send = mlp_forward(
        normed, w_in, w_out, slot, own.reshape(-1, width), scale, regions, rows
    )
    h_got = swap_core(h_send)
    s_got = swap_core(s_send)
    g_in, g_region, dblock, count = mlp_backward(known, slot, scale, w_out, slope, regions)
    g_other = swap_core(g_in)
    dconv, narrow = norm_backward(g_in, w_in, full, inv)
    halves = weight_gradient(g_in, g_other, normed, normed_other, h_mine, h_got, s_mine, s_got)
    per = regions // rows
    part, part_send = kernel_gradient(padded, edges, dconv)
    part = part + swap_core(part_send)
    order = orders(bits, 1)
    part_got = exchange(part, (1 << order[0][0], 1 << order[1][0]))
    parts = []
    for k in range(len(CHUNKS)):
        keep, send = halves[2 * k : 2 * k + 2]
        order = orders(bits, k)
        for step in range(bits):
            got = exchange(send, (1 << order[0][step], 1 << order[1][step]))
            if step == bits - 1:
                break
            if k == 0:
                keep, send = halving_round(keep, got, per)
            else:
                left = rows >> (step + 2)
                keep, send, part = tapped_round(keep, got, part, part_got, left, per)
                part_got = None
        parts += [keep, got]

    narrow = narrow.reshape(height, breadth, width)
    d_other, d_near, d_far = halo(narrow, narrow)
    _, back = local_convolution(dconv, d_other, taps, flipped=True)
    grad_image = back_convolution(d_near, d_far, taps, back, dblock)

    per_core = total // rows // 2
    grad_w_out, mine, send = finish(parts, part, g_region, count, per, per_core)
    got = swap_core(send)
    grad_w_in, region_pool, grad_kernel = place_outputs(mine, got, per_core, owned, per)
    return (region_pool, grad_image, grad_w_in.T, grad_w_out, grad_kernel)


def solution(mesh):
    placed = (
        P(("slides", "row"), "col", None),
        P(),
        P(),
        P(),
        P(),
        P(("slides", "row"), "col"),
        P("slides"),
        P(("slides", "row", "col"), None),
    )
    return jax.shard_map(
        compute,
        mesh=mesh,
        in_specs=placed,
        out_specs=(
            P(("slides", "row", "col"), None),
            P(("slides", "row"), "col", None),
            P("slides", ("row", "col")),
            P(("slides", "row", "col"), None),
            P("slides", None),
        ),
        check_vma=False,
    )
```

```python
import functools
import math

import jax
import jax.numpy as jnp
from jax import lax
from jax.experimental import pallas as pl
from jax.experimental.pallas import tpu as pltpu
from jax.sharding import PartitionSpec as P


AXES = ("row", "col")
F32, BF16 = jnp.float32, jnp.bfloat16
VMEM = pl.BlockSpec(memory_space=pltpu.VMEM)
CONTRACT_ROWS = (((0,), (0,)), ((), ()))
CONTRACT_LANES = (((1,), (1,)), ((), ()))
LEFT = 8


def dot(a, b, dims=(((1,), (0,)), ((), ()))):
    return lax.dot_general(a, b, dims, preferred_element_type=F32)


def iota(shape, dim):
    return lax.broadcasted_iota(jnp.int32, shape, dim)


def call(body, outs, micros, scratch=(), far_in=(), any_in=(), far_out=(), room=8):
    def run(*operands):
        operands = [
            pltpu.with_memory_space_constraint(
                x, pltpu.HBM if k in far_in or k in any_in else pltpu.VMEM
            )
            for k, x in enumerate(operands)
        ]
        specs = [
            pl.BlockSpec(memory_space=pl.ANY) if k in any_in else VMEM
            for k in range(len(operands))
        ]
        shapes = [
            jax.ShapeDtypeStruct(shape, dtype) if k in far_out else pltpu.VMEM(shape, dtype)
            for k, (shape, dtype) in enumerate(outs)
        ]
        return pl.pallas_call(
            body,
            in_specs=specs,
            out_specs=[VMEM] * len(outs),
            out_shape=shapes,
            scratch_shapes=list(scratch),
            compiler_params=pltpu.CompilerParams(vmem_limit_bytes=room << 20),
            cost_estimate=pl.CostEstimate(
                flops=0, bytes_accessed=int(micros * 3.0e6), transcendentals=0
            ),
        )(*operands)

    return run


def exchange(value, chips, flip_core=False):
    rows = lax.axis_size("row")
    pairs = []
    for r in range(rows):
        for c in range(2):
            pairs.append((2 * r + c, 2 * (r ^ chips[c]) + (c ^ int(flip_core))))
    return lax.ppermute(value, AXES, pairs)


def swap_core(value):
    return exchange(value, (0, 0), True)


def swap_rows(value):
    rows = lax.axis_size("row")
    pairs = []
    for r in range(rows - 1):
        pairs.append((2 * r + 1, 2 * r + 2))
        pairs.append((2 * r + 2, 2 * r + 1))
    return lax.ppermute(value, AXES, pairs)


def orders(bits, chunk):
    plain = list(range(bits))
    if bits < 4:
        return plain, plain
    if chunk == 0:
        return [1, 2, 0] + plain[3:], [2, 1, 3, 0] + plain[4:]
    return plain, [0, 3, 1, 2] + plain[4:]


def layout_place(chip, row, core, order):
    value = chip ^ row
    bits = len(order[0])
    out = jnp.zeros_like(value)
    for k in range(bits):
        taken = jnp.where(core == 0, (value >> order[0][k]) & 1, (value >> order[1][k]) & 1)
        out = out | (taken << (bits - 1 - k))
    return out


def prepare_body(
    ids_ref, table_ref, grad_ref, image_ref, taps_ref, scale_ref,
    known_ref, slot_ref, image_out, taps_out, scale_out, sems,
):
    copies = [
        pltpu.make_async_copy(image_ref, image_out, sems.at[0]),
        pltpu.make_async_copy(taps_ref, taps_out, sems.at[1]),
    ]
    for copy in copies:
        copy.start()
    scale_out[...] = scale_ref[...].reshape(scale_out.shape)
    tall, wide = ids_ref.shape
    regions = table_ref.shape[1]
    tiles = tall * wide
    owned = grad_ref.shape[0]
    eye = iota((wide, wide), 0) == iota((wide, wide), 1)
    columns = []
    for t in range(tall):
        row = jnp.broadcast_to(ids_ref[t : t + 1, :].astype(F32), (wide, wide))
        columns.append(jnp.sum(jnp.where(eye, row, 0.0), axis=1, keepdims=True))
    ids = jnp.concatenate(columns, axis=0)
    match = ids == iota((tiles, regions), 1).astype(F32)
    table = jnp.broadcast_to(table_ref[...].astype(F32), (tiles, regions))
    slot = jnp.sum(jnp.where(match, table, 0.0), axis=1, keepdims=True)
    onehot = (slot == iota((tiles, regions), 1).astype(F32)).astype(F32)
    known_ref[...] = jnp.zeros_like(known_ref)
    known_ref[:owned, :] = grad_ref[...]
    known_ref[owned : owned + 1, :regions] = jnp.sum(onehot, axis=0, keepdims=True).astype(BF16)
    places = tiles * 4
    p = iota((places, tiles), 0)
    line = 2 * wide
    tile = (p // (2 * line)) * wide + (p % line) // 2
    expand = (tile == iota((places, tiles), 1)).astype(F32)
    slot_row = jnp.sum(
        jnp.where(iota((tiles, tiles), 0) == iota((tiles, tiles), 1), slot, 0.0),
        axis=0,
        keepdims=True,
    )
    slot_ref[...] = jnp.sum(expand * slot_row, axis=1, keepdims=True)
    for copy in copies:
        copy.wait()


def prepare(ids, table, grad, image, taps, scale):
    width = grad.shape[1]
    outs = [
        ((8, width), BF16),
        ((4 * ids.size, 1), F32),
        (image.shape, BF16),
        (taps.shape, F32),
        ((1, width), F32),
    ]
    scratch = [pltpu.SemaphoreType.DMA((2,))]
    return call(
        prepare_body, outs, 1.5, scratch, far_in=(0, 1, 2, 5), any_in=(3, 4)
    )(ids, table.reshape(1, -1), grad, image, taps, scale)


def pack_body(own_ref, other_ref, out_ref):
    c = lax.axis_index("col")
    height, breadth, _ = own_ref.shape

    @pl.when(c == 0)
    def _():
        out_ref[:, :breadth] = own_ref[:3]
        out_ref[:, breadth:] = other_ref[:3]

    @pl.when(c == 1)
    def _():
        out_ref[:, :breadth] = other_ref[height - 3 :]
        out_ref[:, breadth:] = own_ref[height - 3 :]


def halo(source, field):
    _, breadth, width = field.shape
    other = swap_core(source)
    (packed,) = call(pack_body, [((3, 2 * breadth, width), field.dtype)], 0.5)(field, other)
    near = swap_rows(packed)
    far = swap_core(near)
    return other, near, far


def fill_center(pad_ref, own_ref, other_ref):
    c = lax.axis_index("col")
    height, breadth, lanes = other_ref.shape
    stop = LEFT + breadth
    for i in range(height):
        if len(own_ref.shape) == 3:
            own = own_ref[i]
        else:
            own = own_ref[i * breadth : (i + 1) * breadth, :]
        pad_ref[i, LEFT:stop, :] = own.astype(F32)

    @pl.when(c == 0)
    def _():
        pad_ref[:, stop : stop + 8, :] = other_ref[:, :8, :].astype(F32)
        pad_ref[:, :LEFT, :] = jnp.zeros((height, LEFT, lanes), F32)

    @pl.when(c == 1)
    def _():
        pad_ref[:, :LEFT, :] = other_ref[:, breadth - 8 :, :].astype(F32)
        pad_ref[:, stop : stop + 8, :] = jnp.zeros((height, 8, lanes), F32)


def fill_edges(edge_ref, near_ref, far_ref):
    c = lax.axis_index("col")
    breadth, lanes = near_ref.shape[1] // 2, near_ref.shape[2]
    stop = LEFT + breadth

    @pl.when(c == 0)
    def _():
        edge_ref[:3, LEFT : stop + 8, :] = near_ref[:, : breadth + 8, :].astype(F32)
        edge_ref[3:, LEFT : stop + 8, :] = far_ref[:, : breadth + 8, :].astype(F32)
        edge_ref[:, :LEFT, :] = jnp.zeros((6, LEFT, lanes), F32)

    @pl.when(c == 1)
    def _():
        edge_ref[:3, :stop, :] = far_ref[:, breadth - 8 :, :].astype(F32)
        edge_ref[3:, :stop, :] = near_ref[:, breadth - 8 :, :].astype(F32)
        edge_ref[:, stop : stop + 8, :] = jnp.zeros((6, 8, lanes), F32)


def convolve(lines, sums, taps_ref, breadth, lanes, flipped):
    sums = list(sums)
    height = len(sums)
    for b in range(7):
        start = LEFT - 3 + b
        for ref, at, i in lines:
            line = ref[at, start : start + breadth, lanes]
            for a in range(7):
                row = i - a
                if 0 <= row < height:
                    tap = 48 - (7 * a + b) if flipped else 7 * a + b
                    term = line * taps_ref[tap : tap + 1, lanes]
                    sums[row] = term if sums[row] is None else sums[row] + term
    return sums


def center_lines(ref):
    return [(ref, i, i + 3) for i in range(ref.shape[0])]


def edge_lines(ref, height):
    return [(ref, i, i) for i in range(3)] + [(ref, i + 3, i + height + 3) for i in range(3)]


def over_lanes(width, block):
    def step(k, carry):
        for side in range(2):
            block(pl.ds(pl.multiple_of(k * 256 + side * 128, 128), 128))
        return carry

    lax.fori_loop(0, width // 256, step, 0)


def local_body(flipped, copied, *refs):
    own_ref, other_ref, taps_ref = refs[:3]
    sources = refs[3 : 3 + copied]
    pad_ref, sum_ref = refs[3 + copied : 5 + copied]
    targets = refs[5 + copied : 5 + 2 * copied]
    copies = []
    for k in range(copied):
        copies.append(pltpu.make_async_copy(sources[k], targets[k], refs[-1].at[k]))
        copies[k].start()
    height, breadth, width = other_ref.shape
    fill_center(pad_ref, own_ref, other_ref)

    def block(lanes):
        sums = convolve(
            center_lines(pad_ref), [None] * height, taps_ref, breadth, lanes, flipped
        )
        for i, row in enumerate(sums):
            sum_ref[i * breadth : (i + 1) * breadth, lanes] = row

    over_lanes(width, block)
    for copy in copies:
        copy.wait()


def local_convolution(own, other, taps, flipped=False, copied=()):
    height, breadth, width = other.shape
    outs = [((height, breadth + 16, width), F32), ((height * breadth, width), F32)]
    outs += [(x.shape, x.dtype) for x in copied]
    scratch = [pltpu.SemaphoreType.DMA((len(copied),))] if copied else []
    return call(
        functools.partial(local_body, flipped, len(copied)),
        outs,
        4.0,
        scratch,
        any_in=tuple(range(3, 3 + len(copied))),
    )(own, other, taps, *copied)


def conv_norm_body(
    near_ref, far_ref, taps_ref, sum_ref, edge_ref, normed_ref, send_ref, full_ref, inv_ref
):
    places, width = sum_ref.shape
    breadth = near_ref.shape[1] // 2
    height = places // breadth
    steps, half = width // 128, width // 2
    fill_edges(edge_ref, near_ref, far_ref)

    for k in range(0, width, 128):
        lanes = slice(k, k + 128)
        sums = [sum_ref[i * breadth : (i + 1) * breadth, lanes] for i in range(height)]
        sums = convolve(edge_lines(edge_ref, height), sums, taps_ref, breadth, lanes, False)
        for i, row in enumerate(sums):
            full_ref[i * breadth : (i + 1) * breadth, lanes] = row

    for i in range(0, places, 16):
        rows = slice(i, i + 16)
        parts = [full_ref[rows, s * 128 : (s + 1) * 128] for s in range(steps)]
        mean = jnp.sum(functools.reduce(jnp.add, parts), axis=1, keepdims=True) * (1.0 / width)
        parts = [p - mean for p in parts]
        total = functools.reduce(jnp.add, [p * p for p in parts])
        var = jnp.sum(total, axis=1, keepdims=True) * (1.0 / width)
        inv = lax.rsqrt(var + 1e-06)
        inv_ref[rows, :] = jnp.broadcast_to(inv, (16, 128))
        for s, p in enumerate(parts):
            value = p * inv
            full_ref[rows, s * 128 : (s + 1) * 128] = value
            normed_ref[rows, s * 128 : (s + 1) * 128] = value.astype(BF16)
    c = lax.axis_index("col")
    send_ref[...] = normed_ref[:, pl.ds(pl.multiple_of((1 - c) * half, 128), half)]


def conv_norm(near, far, taps, sums):
    places, width = sums.shape
    outs = [
        ((6, near.shape[1] // 2 + 16, width), F32),
        ((places, width), BF16),
        ((places, width // 2), BF16),
        ((places, width), F32),
        ((places, 128), F32),
    ]
    return call(conv_norm_body, outs, 5.0)(near, far, taps, sums)


def lane_pack(rows, stack):
    _, wide = rows.shape
    tall = jnp.concatenate([rows[:, s : s + 128] for s in range(0, wide, 128)], axis=0)
    each = tall.shape[0] // stack
    return jnp.concatenate([tall[s * each : (s + 1) * each] for s in range(stack)], axis=1)


def lane_unpack(packed, n):
    _, wide = packed.shape
    tall = jnp.concatenate([packed[:, s : s + 128] for s in range(0, wide, 128)], axis=0)
    count = tall.shape[0] // n
    return jnp.concatenate([tall[s * n : (s + 1) * n] for s in range(count)], axis=1)


UNITS = 768


def forward_body(
    rows, normed_ref, w_in_ref, w_out_ref, slot_ref, image_ref, scale_ref,
    slope_ref, h_mine_ref, h_send_ref, s_mine_ref, s_send_ref, pre, hidden, branch, block,
):
    c = lax.axis_index("col")
    places, width = branch.shape
    total = w_in_ref.shape[1]
    regions = s_mine_ref.shape[0]
    half = width // 2
    per_chip = total // rows
    per_core = per_chip // 2
    slot = slot_ref[...]
    select = (slot == iota((places, regions), 1).astype(F32)).astype(BF16)
    blocks = total // UNITS

    def expand(f):
        pre[f % 2] = dot(normed_ref[...], w_in_ref[:, f * UNITS : (f + 1) * UNITS])

    def activate(f):
        for row in range(0, places, 16):
            line = slice(row, row + 16)
            for start in range(0, UNITS, 256):
                value = pre[f % 2, line, start : start + 256]
                cdf = 0.5 * (1.0 + lax.erf(value * (1.0 / math.sqrt(2.0))))
                density = jnp.exp(-0.5 * value * value) * (1.0 / math.sqrt(2.0 * math.pi))
                hidden[f % 2, line, start : start + 256] = (value * cdf).astype(BF16)
                at = f * UNITS + start
                slope_ref[line, at : at + 256] = cdf + value * density

    def reduce(f):
        part = dot(hidden[f % 2], w_out_ref[f * UNITS : (f + 1) * UNITS, :])
        branch[...] = part if f == 0 else branch[...] + part
        by_region = dot(hidden[f % 2], select, CONTRACT_ROWS)
        for t in range(UNITS // per_chip):
            q = f * (UNITS // per_chip) + t
            low = by_region[t * per_chip : t * per_chip + per_core]
            high = by_region[t * per_chip + per_core : (t + 1) * per_chip]
            h_mine_ref[q] = lane_pack(jnp.where(c == 0, low, high), half // 128)
            h_send_ref[q] = lane_pack(jnp.where(c == 0, high, low), half // 128).astype(BF16)

    expand(0)
    for f in range(blocks):
        if f + 1 < blocks:
            expand(f + 1)
        activate(f)
        reduce(f)
    block[...] = (image_ref[...].astype(F32) + scale_ref[...] * branch[...]).astype(BF16)
    for at, out in ((c, s_mine_ref), (1 - c, s_send_ref)):
        columns = block[:, pl.ds(pl.multiple_of(at * half, 128), half)]
        out[...] = dot(select, columns, CONTRACT_ROWS)


def mlp_forward(normed, w_in, w_out, slot, image, scale, regions, rows):
    places, width = normed.shape
    total, half = w_in.shape[1], width // 2
    packed = total // rows // 2 * regions // half
    outs = [
        ((places, total), F32),
        ((rows, packed, half), F32),
        ((rows, packed, half), BF16),
        ((regions, half), F32),
        ((regions, half), F32),
    ]
    scratch = [
        pltpu.VMEM((2, places, UNITS), F32),
        pltpu.VMEM((2, places, UNITS), BF16),
        pltpu.VMEM((places, width), F32),
        pltpu.VMEM((places, width), BF16),
    ]
    return call(functools.partial(forward_body, rows), outs, 9.0, scratch, room=12)(
        normed, w_in, w_out, slot, image, scale
    )


def backward_body(
    *refs,
):
    known_refs = refs[:4]
    slot_ref, scale_ref, w_out_ref, slope_ref = refs[4:8]
    g_in_ref, region_ref, dblock_ref, count_ref, g_out, known_all = refs[8:]
    r, c = lax.axis_index("row"), lax.axis_index("col")
    me = 2 * r + c
    places, units = slope_ref.shape
    regions = region_ref.shape[0]
    piece = known_refs[0].shape[0]
    for k in range(4):
        known_all[k * piece : (k + 1) * piece, :] = known_refs[k][...]
    total = 4 * piece
    owned = regions * 8 // total
    known = known_all[...]
    is_count = (iota((total, 128), 0) & 7) == owned
    count = dot(known[:, :regions], is_count.astype(BF16), CONTRACT_ROWS)
    count_ref[...] = count
    line = iota((regions, total), 1)
    bits = (total >> 4).bit_length() - 1
    source = gathered_device(line >> 3, me, bits) * owned + (line & 7)
    place = ((line & 7) < owned) & (source == iota((regions, total), 0))
    pooled = dot(place.astype(BF16), known)
    region_grad = (pooled / (4.0 * count[:, :1])).astype(BF16)
    g_region = (region_grad.astype(F32) * scale_ref[...]).astype(BF16)
    region_ref[...] = g_region
    select = (slot_ref[...] == iota((places, regions), 1).astype(F32)).astype(BF16)
    g_out[...] = dot(select, g_region).astype(BF16)
    dblock_ref[...] = dot(select, region_grad).astype(BF16)

    for f in range(0, units, UNITS):
        at = slice(f, f + UNITS)
        dhidden = dot(g_out[...], w_out_ref[at, :], CONTRACT_LANES)
        g_in_ref[:, at] = (dhidden * slope_ref[:, at]).astype(BF16)


def mlp_backward(known, slot, scale, w_out, slope, regions):
    places, total = slope.shape
    width = w_out.shape[1]
    outs = [
        ((places, total), BF16),
        ((regions, width), BF16),
        ((places, width), BF16),
        ((regions, 128), F32),
    ]
    scratch = [
        pltpu.VMEM((places, width), BF16),
        pltpu.VMEM((4 * known[0].shape[0], width), BF16),
    ]
    return call(backward_body, outs, 4.0, scratch)(
        *known, slot, scale, w_out, slope
    )


def norm_backward_body(g_in_ref, w_in_ref, full_ref, inv_ref, dconv_ref, narrow_ref):
    places, width = dconv_ref.shape
    dconv_ref[...] = dot(g_in_ref[...], w_in_ref[...], CONTRACT_LANES)

    for i in range(0, places, 16):
        rows = slice(i, i + 16)
        lanes = [slice(s, s + 128) for s in range(0, width, 128)]
        grads = [dconv_ref[rows, at] for at in lanes]
        fulls = [full_ref[rows, at] for at in lanes]
        mean = jnp.sum(functools.reduce(jnp.add, grads), axis=1, keepdims=True) * (1.0 / width)
        total = functools.reduce(jnp.add, [g * n for g, n in zip(grads, fulls)])
        along = jnp.sum(total, axis=1, keepdims=True) * (1.0 / width)
        inv = inv_ref[rows, :]
        for at, g, n in zip(lanes, grads, fulls):
            value = inv * (g - mean - n * along)
            dconv_ref[rows, at] = value
            narrow_ref[rows, at] = value.astype(BF16)


def norm_backward(g_in, w_in, full, inv):
    places, width = full.shape
    outs = [((places, width), F32), ((places, width), BF16)]
    return call(norm_backward_body, outs, 4.0)(g_in, w_in, full, inv)


def split_high_low(value):
    high = value.astype(BF16)
    return high, (value - high.astype(F32)).astype(BF16)


CHUNKS = ((0, 256), (256, 128))


def weight_body(
    rows, own_ref, other_ref, normed_ref, normed_other_ref, h_mine_ref, h_got_ref, s_mine_ref,
    s_got_ref, *out_refs,
):
    r, c = lax.axis_index("row"), lax.axis_index("col")
    bits = rows.bit_length() - 1
    half = h_mine_ref.shape[2]
    total = own_ref.shape[1]
    count = rows // 2
    per_chip = total // rows
    packed = h_mine_ref.shape[1]
    per = s_mine_ref.shape[0] // rows
    columns = pl.ds(pl.multiple_of(c * half, 128), half)

    def store(q, value, first):
        for k, (lane, wide) in enumerate(CHUNKS):
            j = layout_place(jnp.int32(q), r, c, orders(bits, k))
            out_refs[2 * k][j, first : first + value.shape[0], :] = value[:, lane : lane + wide]

    for q in range(rows):
        store(q, h_mine_ref[q] + h_got_ref[q].astype(F32), per_chip)
        at = slice(q * per, (q + 1) * per)
        store(q, s_mine_ref[at, :] + s_got_ref[at, :], per_chip + packed)
    for f in range(0, total, UNITS):
        at = slice(f, f + UNITS)
        grad = dot(own_ref[:, at], normed_ref[:, columns], CONTRACT_ROWS)
        grad += dot(other_ref[:, at], normed_other_ref[...], CONTRACT_ROWS)
        for t in range(UNITS // per_chip):
            store((f + t * per_chip) // per_chip, grad[t * per_chip : (t + 1) * per_chip], 0)
    body = per_chip + packed
    for k in range(len(CHUNKS)):
        all_ref, send_ref = out_refs[2 * k : 2 * k + 2]
        for j in range(count):
            send_ref[j, :body, :] = all_ref[count + j, :body, :].astype(BF16)
            sums = all_ref[count + j, body:, :]
            send_ref[j, body:, :] = jnp.concatenate(split_high_low(sums), axis=0)


def weight_gradient(g_in, g_other, normed, normed_other, h_mine, h_got, s_mine, s_got):
    total = g_in.shape[1]
    rows, packed, _ = h_mine.shape
    per = s_mine.shape[0] // rows
    height = total // rows + packed + per
    outs = []
    for _, wide in CHUNKS:
        outs.append(((rows, height, wide), F32))
        outs.append(((rows // 2, height + per, wide), BF16))
    return call(functools.partial(weight_body, rows), outs, 5.0, room=12)(
        g_in, g_other, normed, normed_other, h_mine, h_got, s_mine, s_got
    )


def merged(keep, got, per):
    body = keep.shape[0] - per
    plain = keep[:body] + got[:body].astype(F32)
    sums = keep[body:] + (got[body : body + per].astype(F32) + got[body + per :].astype(F32))
    return plain, sums


def round_body(per, old_ref, got_ref, keep_ref, send_ref):
    left = keep_ref.shape[0]
    body = keep_ref.shape[1] - per

    def near(i, carry):
        plain, sums = merged(old_ref[i], got_ref[i], per)
        keep_ref[i, :body, :] = plain
        keep_ref[i, body:, :] = sums
        return carry

    def far(i, carry):
        plain, sums = merged(old_ref[i + left], got_ref[i + left], per)
        send_ref[i, :body, :] = plain.astype(BF16)
        send_ref[i, body:, :] = jnp.concatenate(split_high_low(sums), axis=0)
        return carry

    lax.fori_loop(0, left, far, 0)
    lax.fori_loop(0, left, near, 0)


def halving_round(keep, got, per):
    _, height, wide = keep.shape
    left = got.shape[0] // 2
    outs = [((left, height, wide), F32), ((left, height + per, wide), BF16)]
    return call(functools.partial(round_body, per), outs, 0.5)(keep, got)


def taps_to_rows(taps):
    return jnp.concatenate(
        [taps[:, k : k + 128] for k in range(0, taps.shape[1], 128)], axis=0
    )


def rows_to_taps(rows, count):
    pieces = [rows[k : k + count] for k in range(0, rows.shape[0], count)]
    return jnp.concatenate(pieces, axis=1)


def taps_received(got_ref, first, count):
    return rows_to_taps(got_ref[first:, :].astype(F32), count)


def tapped_round_body(
    per, carried, old_ref, got_ref, taps_ref, taps_got_ref, keep_ref, send_ref, taps_out_ref
):
    left = keep_ref.shape[0]
    height = keep_ref.shape[1] + per
    body = keep_ref.shape[1] - per

    def block(i):
        at = pl.ds(pl.multiple_of(i * height, 16), height)
        return merged(old_ref[i], got_ref[at, :], per)

    def near(i, carry):
        plain, sums = block(i)
        keep_ref[i, :body, :] = plain
        keep_ref[i, body:, :] = sums
        return carry

    def far(i, carry):
        plain, sums = block(i + left)
        send_ref[pl.ds(pl.multiple_of(i * height, 16), body), :] = plain.astype(BF16)
        tail = pl.ds(pl.multiple_of(i * height + body, 16), 2 * per)
        send_ref[tail, :] = jnp.concatenate(split_high_low(sums), axis=0)
        return carry

    lax.fori_loop(0, left, far, 0)
    count = taps_ref.shape[0]
    if carried:
        taps = taps_ref[...] + taps_received(got_ref, 2 * left * height, count)
    else:
        taps = taps_ref[...] + taps_got_ref[...]
    taps_out_ref[...] = taps.astype(BF16).astype(F32)
    send_ref[left * height :, :] = taps_to_rows(taps).astype(BF16)
    lax.fori_loop(0, left, near, 0)


def tapped_round(keep, got, taps, taps_got, left, per):
    _, height, wide = keep.shape
    rows = taps.size // wide
    outs = [
        ((left, height, wide), F32),
        ((left * (height + per) + rows, wide), BF16),
        (taps.shape, F32),
    ]
    carried = taps_got is None
    body = functools.partial(tapped_round_body, per, carried)
    return call(body, outs, 0.5)(keep, got.reshape(-1, wide), taps, taps if carried else taps_got)


def finish_body(per, *refs):
    keep_a, got_a, keep_b, got_b, taps_ref, region_ref, count_ref = refs[:7]
    out_ref, mine_ref, send_ref = refs[7:]
    r, c = lax.axis_index("row"), lax.axis_index("col")
    height = keep_b.shape[1] + per
    done = [merged(keep_a[0], got_a[0], per), merged(keep_b[0], got_b[:height, :], per)]
    plain = jnp.concatenate([d[0] for d in done], axis=1)
    sums = jnp.concatenate([d[1] for d in done], axis=1)
    per_core = out_ref.shape[0]
    half = plain.shape[1]
    first, second = plain[:per_core], plain[per_core : 2 * per_core]
    high, low = split_high_low(lane_unpack(plain[2 * per_core :], per_core))
    out_ref[...] = dot(high, region_ref[...]) + dot(low, region_ref[...])
    mine_ref[:per_core, :] = jnp.where(c == 0, first, second)
    send_ref[:per_core, :] = jnp.where(c == 0, second, first)
    start = pl.multiple_of(r * per, per)
    pooled = sums / (4.0 * count_ref[pl.ds(start, per), :1])
    count = taps_ref.shape[0]
    taps = taps_ref[...] + taps_received(got_b, height, count)
    for ref in (mine_ref, send_ref):
        ref[per_core : per_core + per, :] = pooled
        ref[per_core + per : per_core + per + count, :] = taps[:, :half]
        ref[per_core + per + count :, :] = taps[:, half:]


def finish(parts, taps, region, count, per, per_core):
    width = region.shape[1]
    part = ((per_core + per + 2 * taps.shape[0], width // 2), F32)
    outs = [((per_core, width), F32), part, part]
    return call(functools.partial(finish_body, per), outs, 1.0, far_out=(0,))(
        *parts, taps, region, count
    )


def place_body(per, mine_ref, got_ref, grad_ref, pool_ref, taps_ref):
    c = lax.axis_index("col")
    per_core, width = grad_ref.shape
    half = width // 2
    owned = pool_ref.shape[0]
    first = per_core + per
    count = (mine_ref.shape[0] - first) // 2
    for core in range(2):

        @pl.when(c == core)
        def _():
            left, right = (mine_ref, got_ref) if core == 0 else (got_ref, mine_ref)
            grad_ref[:, :half] = left[:per_core, :]
            grad_ref[:, half:] = right[:per_core, :]
            rows = slice(per_core + core * owned, per_core + (core + 1) * owned)
            pool_ref[:, :half] = left[rows, :]
            pool_ref[:, half:] = right[rows, :]
            for k in range(2):
                at = slice(k * half, (k + 1) * half)
                low = first + k * count
                taps_ref[:28, at] = left[low : low + 28, :]
                taps_ref[28:, at] = right[low : low + 21, :]


def place_outputs(mine, got, per_core, owned, per):
    width = 2 * mine.shape[1]
    outs = [((per_core, width), F32), ((owned, width), F32), ((49, width), F32)]
    return call(functools.partial(place_body, per), outs, 0.5, far_out=(0, 1, 2))(mine, got)


def kernel_gradient_body(pad_ref, edge_ref, dconv_ref, mine_ref, send_ref):
    c = lax.axis_index("col")
    height, wide, width = pad_ref.shape
    breadth = wide - 16

    def block(lanes):
        sums = {}
        grads = [dconv_ref[i * breadth : (i + 1) * breadth, lanes] for i in range(height)]
        for b in range(7):
            start = LEFT - 3 + b
            for ref, at, i in center_lines(pad_ref) + edge_lines(edge_ref, height):
                line = ref[at, start : start + breadth, lanes]
                for a in range(7):
                    row = i - a
                    if 0 <= row < height:
                        term = (line * grads[row]).reshape(breadth // 8, 8, 128).sum(axis=0)
                        sums[a, b] = sums[a, b] + term if (a, b) in sums else term
            for a in range(7):
                sums[a, b] = jnp.sum(sums[a, b], axis=0, keepdims=True)

        def put(ref, first, last):
            ref[24:, lanes] = jnp.zeros((8, 128), F32)
            for a in range(first, last):
                for b in range(7):
                    at = (a - first) * 7 + b
                    ref[at : at + 1, lanes] = sums[a, b]

        @pl.when(c == 0)
        def _():
            put(mine_ref, 0, 4)
            put(send_ref, 4, 7)

        @pl.when(c == 1)
        def _():
            put(mine_ref, 4, 7)
            put(send_ref, 0, 4)

    over_lanes(width, block)


def kernel_gradient(padded, edges, dconv):
    width = dconv.shape[1]
    outs = [((32, width), F32)] * 2
    return call(kernel_gradient_body, outs, 5.0)(padded, edges, dconv)


def back_body(near_ref, far_ref, taps_ref, sum_ref, dblock_ref, out_ref, edge_ref):
    height, breadth, width = out_ref.shape
    fill_edges(edge_ref, near_ref, far_ref)

    def block(lanes):
        sums = [sum_ref[i * breadth : (i + 1) * breadth, lanes] for i in range(height)]
        sums = convolve(edge_lines(edge_ref, height), sums, taps_ref, breadth, lanes, True)
        for i, row in enumerate(sums):
            rows = slice(i * breadth, (i + 1) * breadth)
            out_ref[i, :, lanes] = (dblock_ref[rows, lanes].astype(F32) + row).astype(BF16)

    over_lanes(width, block)


def back_convolution(near, far, taps, sums, dblock):
    places, width = sums.shape
    breadth = near.shape[1] // 2
    outs = [((places // breadth, breadth, width), BF16)]
    scratch = [pltpu.VMEM((6, breadth + 16, width), F32)]
    (out,) = call(back_body, outs, 3.0, scratch, far_out=(0,))(near, far, taps, sums, dblock)
    return out


def gather_stages(bits):
    return list(range((bits - 1) // 2 * 2, -1, -2))


def gather_known(known):
    bits = lax.axis_size("row").bit_length() - 1
    pieces = [known, swap_core(known)]
    for low in gather_stages(bits):
        known = jnp.concatenate(pieces, axis=0)
        pieces = [known]
        for mask in (1 << low, 2 << low, 3 << low):
            pieces.append(exchange(known, (mask, mask)))
    return pieces


def gathered_device(block, me, bits):
    mask = block & 1
    for k, low in enumerate(gather_stages(bits)):
        mask = mask | (((block >> (2 * k + 1)) & 3) << (low + 1))
    return me ^ mask


def compute(image, dw_kernel, w_in, w_out, layer_scale, region_ids, region_slot, pool_grad):
    height, breadth, width = image.shape
    total = w_in.shape[1]
    rows = lax.axis_size("row")
    bits = rows.bit_length() - 1
    regions = region_slot.shape[0]
    owned = pool_grad.shape[0]
    known, slot, own, taps, scale = prepare(
        region_ids, region_slot, pool_grad, image, dw_kernel, layer_scale
    )
    other, near, far = halo(image, own)
    known = gather_known(known)

    padded, sums, w_in, w_out = local_convolution(own, other, taps, copied=(w_in, w_out))
    edges, normed, normed_send, full, inv = conv_norm(near, far, taps, sums)
    normed_other = swap_core(normed_send)
    slope, h_mine, h_send, s_mine, s_send = mlp_forward(
        normed, w_in, w_out, slot, own.reshape(-1, width), scale, regions, rows
    )
    h_got = swap_core(h_send)
    s_got = swap_core(s_send)
    g_in, g_region, dblock, count = mlp_backward(known, slot, scale, w_out, slope, regions)
    g_other = swap_core(g_in)
    dconv, narrow = norm_backward(g_in, w_in, full, inv)
    halves = weight_gradient(g_in, g_other, normed, normed_other, h_mine, h_got, s_mine, s_got)
    per = regions // rows
    part, part_send = kernel_gradient(padded, edges, dconv)
    part = part + swap_core(part_send)
    order = orders(bits, 1)
    part_got = exchange(part, (1 << order[0][0], 1 << order[1][0]))
    parts = []
    for k in range(len(CHUNKS)):
        keep, send = halves[2 * k : 2 * k + 2]
        order = orders(bits, k)
        for step in range(bits):
            got = exchange(send, (1 << order[0][step], 1 << order[1][step]))
            if step == bits - 1:
                break
            if k == 0:
                keep, send = halving_round(keep, got, per)
            else:
                left = rows >> (step + 2)
                keep, send, part = tapped_round(keep, got, part, part_got, left, per)
                part_got = None
        parts += [keep, got]

    narrow = narrow.reshape(height, breadth, width)
    d_other, d_near, d_far = halo(narrow, narrow)
    _, back = local_convolution(dconv, d_other, taps, flipped=True)
    grad_image = back_convolution(d_near, d_far, taps, back, dblock)

    per_core = total // rows // 2
    grad_w_out, mine, send = finish(parts, part, g_region, count, per, per_core)
    got = swap_core(send)
    grad_w_in, region_pool, grad_kernel = place_outputs(mine, got, per_core, owned, per)
    return (region_pool, grad_image, grad_w_in.T, grad_w_out, grad_kernel)


def solution(mesh):
    placed = (
        P(("slides", "row"), "col", None),
        P(),
        P(),
        P(),
        P(),
        P(("slides", "row"), "col"),
        P("slides"),
        P(("slides", "row", "col"), None),
    )
    return jax.shard_map(
        compute,
        mesh=mesh,
        in_specs=placed,
        out_specs=(
            P(("slides", "row", "col"), None),
            P(("slides", "row"), "col", None),
            P("slides", ("row", "col")),
            P(("slides", "row", "col"), None),
            P("slides", None),
        ),
        check_vma=False,
    )
```

```python
import functools
import math

import jax
import jax.numpy as jnp
from jax import lax
from jax.experimental import pallas as pl
from jax.experimental.pallas import tpu as pltpu
from jax.sharding import PartitionSpec as P


AXES = ("row", "col")
F32, BF16 = jnp.float32, jnp.bfloat16
VMEM = pl.BlockSpec(memory_space=pltpu.VMEM)
CONTRACT_ROWS = (((0,), (0,)), ((), ()))
CONTRACT_LANES = (((1,), (1,)), ((), ()))
LEFT = 8


def dot(a, b, dims=(((1,), (0,)), ((), ()))):
    return lax.dot_general(a, b, dims, preferred_element_type=F32)


def iota(shape, dim):
    return lax.broadcasted_iota(jnp.int32, shape, dim)


def call(body, outs, micros, scratch=(), far_in=(), any_in=(), far_out=(), room=8):
    def run(*operands):
        operands = [
            pltpu.with_memory_space_constraint(
                x, pltpu.HBM if k in far_in or k in any_in else pltpu.VMEM
            )
            for k, x in enumerate(operands)
        ]
        specs = [
            pl.BlockSpec(memory_space=pl.ANY) if k in any_in else VMEM
            for k in range(len(operands))
        ]
        shapes = [
            jax.ShapeDtypeStruct(shape, dtype) if k in far_out else pltpu.VMEM(shape, dtype)
            for k, (shape, dtype) in enumerate(outs)
        ]
        return pl.pallas_call(
            body,
            in_specs=specs,
            out_specs=[VMEM] * len(outs),
            out_shape=shapes,
            scratch_shapes=list(scratch),
            compiler_params=pltpu.CompilerParams(vmem_limit_bytes=room << 20),
            cost_estimate=pl.CostEstimate(
                flops=0, bytes_accessed=int(micros * 3.0e6), transcendentals=0
            ),
        )(*operands)

    return run


def exchange(value, chips, flip_core=False):
    rows = lax.axis_size("row")
    pairs = []
    for r in range(rows):
        for c in range(2):
            pairs.append((2 * r + c, 2 * (r ^ chips[c]) + (c ^ int(flip_core))))
    return lax.ppermute(value, AXES, pairs)


def swap_core(value):
    return exchange(value, (0, 0), True)


def swap_rows(value):
    rows = lax.axis_size("row")
    pairs = []
    for r in range(rows - 1):
        pairs.append((2 * r + 1, 2 * r + 2))
        pairs.append((2 * r + 2, 2 * r + 1))
    return lax.ppermute(value, AXES, pairs)


def orders(bits, chunk):
    plain = list(range(bits))
    if bits < 4:
        return plain, plain
    if chunk == 0:
        return [1, 2, 0] + plain[3:], [2, 1, 3, 0] + plain[4:]
    return plain, [0, 3, 1, 2] + plain[4:]


def layout_place(chip, row, core, order):
    value = chip ^ row
    bits = len(order[0])
    out = jnp.zeros_like(value)
    for k in range(bits):
        taken = jnp.where(core == 0, (value >> order[0][k]) & 1, (value >> order[1][k]) & 1)
        out = out | (taken << (bits - 1 - k))
    return out


def prepare_body(
    ids_ref, table_ref, grad_ref, image_ref, taps_ref, scale_ref,
    known_ref, slot_ref, image_out, taps_out, scale_out, sems,
):
    copies = [
        pltpu.make_async_copy(image_ref, image_out, sems.at[0]),
        pltpu.make_async_copy(taps_ref, taps_out, sems.at[1]),
    ]
    for copy in copies:
        copy.start()
    scale_out[...] = scale_ref[...].reshape(scale_out.shape)
    tall, wide = ids_ref.shape
    regions = table_ref.shape[1]
    tiles = tall * wide
    owned = grad_ref.shape[0]
    eye = iota((wide, wide), 0) == iota((wide, wide), 1)
    columns = []
    for t in range(tall):
        row = jnp.broadcast_to(ids_ref[t : t + 1, :].astype(F32), (wide, wide))
        columns.append(jnp.sum(jnp.where(eye, row, 0.0), axis=1, keepdims=True))
    ids = jnp.concatenate(columns, axis=0)
    match = ids == iota((tiles, regions), 1).astype(F32)
    table = jnp.broadcast_to(table_ref[...].astype(F32), (tiles, regions))
    slot = jnp.sum(jnp.where(match, table, 0.0), axis=1, keepdims=True)
    onehot = (slot == iota((tiles, regions), 1).astype(F32)).astype(F32)
    known_ref[...] = jnp.zeros_like(known_ref)
    known_ref[:owned, :] = grad_ref[...]
    known_ref[owned : owned + 1, :regions] = jnp.sum(onehot, axis=0, keepdims=True).astype(BF16)
    places = tiles * 4
    p = iota((places, tiles), 0)
    line = 2 * wide
    tile = (p // (2 * line)) * wide + (p % line) // 2
    expand = (tile == iota((places, tiles), 1)).astype(F32)
    slot_row = jnp.sum(
        jnp.where(iota((tiles, tiles), 0) == iota((tiles, tiles), 1), slot, 0.0),
        axis=0,
        keepdims=True,
    )
    slot_ref[...] = jnp.sum(expand * slot_row, axis=1, keepdims=True)
    for copy in copies:
        copy.wait()


def prepare(ids, table, grad, image, taps, scale):
    width = grad.shape[1]
    outs = [
        ((8, width), BF16),
        ((4 * ids.size, 1), F32),
        (image.shape, BF16),
        (taps.shape, F32),
        ((1, width), F32),
    ]
    scratch = [pltpu.SemaphoreType.DMA((2,))]
    return call(
        prepare_body, outs, 1.5, scratch, far_in=(0, 1, 2, 5), any_in=(3, 4)
    )(ids, table.reshape(1, -1), grad, image, taps, scale)


def pack_body(own_ref, other_ref, out_ref):
    c = lax.axis_index("col")
    height, breadth, _ = own_ref.shape

    @pl.when(c == 0)
    def _():
        out_ref[:, :breadth] = own_ref[:3]
        out_ref[:, breadth:] = other_ref[:3]

    @pl.when(c == 1)
    def _():
        out_ref[:, :breadth] = other_ref[height - 3 :]
        out_ref[:, breadth:] = own_ref[height - 3 :]


def halo(source, field):
    _, breadth, width = field.shape
    other = swap_core(source)
    (packed,) = call(pack_body, [((3, 2 * breadth, width), field.dtype)], 0.5)(field, other)
    near = swap_rows(packed)
    far = swap_core(near)
    return other, near, far


def fill_center(pad_ref, own_ref, other_ref):
    c = lax.axis_index("col")
    height, breadth, lanes = other_ref.shape
    stop = LEFT + breadth
    for i in range(height):
        if len(own_ref.shape) == 3:
            own = own_ref[i]
        else:
            own = own_ref[i * breadth : (i + 1) * breadth, :]
        pad_ref[i, LEFT:stop, :] = own.astype(F32)

    @pl.when(c == 0)
    def _():
        pad_ref[:, stop : stop + 8, :] = other_ref[:, :8, :].astype(F32)
        pad_ref[:, :LEFT, :] = jnp.zeros((height, LEFT, lanes), F32)

    @pl.when(c == 1)
    def _():
        pad_ref[:, :LEFT, :] = other_ref[:, breadth - 8 :, :].astype(F32)
        pad_ref[:, stop : stop + 8, :] = jnp.zeros((height, 8, lanes), F32)


def fill_edges(edge_ref, near_ref, far_ref):
    c = lax.axis_index("col")
    breadth, lanes = near_ref.shape[1] // 2, near_ref.shape[2]
    stop = LEFT + breadth

    @pl.when(c == 0)
    def _():
        edge_ref[:3, LEFT : stop + 8, :] = near_ref[:, : breadth + 8, :].astype(F32)
        edge_ref[3:, LEFT : stop + 8, :] = far_ref[:, : breadth + 8, :].astype(F32)
        edge_ref[:, :LEFT, :] = jnp.zeros((6, LEFT, lanes), F32)

    @pl.when(c == 1)
    def _():
        edge_ref[:3, :stop, :] = far_ref[:, breadth - 8 :, :].astype(F32)
        edge_ref[3:, :stop, :] = near_ref[:, breadth - 8 :, :].astype(F32)
        edge_ref[:, stop : stop + 8, :] = jnp.zeros((6, 8, lanes), F32)


def convolve(lines, sums, taps_ref, breadth, lanes, flipped):
    sums = list(sums)
    height = len(sums)
    for b in range(7):
        start = LEFT - 3 + b
        for ref, at, i in lines:
            line = ref[at, start : start + breadth, lanes]
            for a in range(7):
                row = i - a
                if 0 <= row < height:
                    tap = 48 - (7 * a + b) if flipped else 7 * a + b
                    term = line * taps_ref[tap : tap + 1, lanes]
                    sums[row] = term if sums[row] is None else sums[row] + term
    return sums


def center_lines(ref):
    return [(ref, i, i + 3) for i in range(ref.shape[0])]


def edge_lines(ref, height):
    return [(ref, i, i) for i in range(3)] + [(ref, i + 3, i + height + 3) for i in range(3)]


def over_lanes(width, block):
    def step(k, carry):
        for side in range(2):
            block(pl.ds(pl.multiple_of(k * 256 + side * 128, 128), 128))
        return carry

    lax.fori_loop(0, width // 256, step, 0)


def local_body(flipped, copied, *refs):
    own_ref, other_ref, taps_ref = refs[:3]
    sources = refs[3 : 3 + copied]
    pad_ref, sum_ref = refs[3 + copied : 5 + copied]
    targets = refs[5 + copied : 5 + 2 * copied]
    copies = []
    for k in range(copied):
        copies.append(pltpu.make_async_copy(sources[k], targets[k], refs[-1].at[k]))
        copies[k].start()
    height, breadth, width = other_ref.shape
    fill_center(pad_ref, own_ref, other_ref)

    def block(lanes):
        sums = convolve(
            center_lines(pad_ref), [None] * height, taps_ref, breadth, lanes, flipped
        )
        for i, row in enumerate(sums):
            sum_ref[i * breadth : (i + 1) * breadth, lanes] = row

    over_lanes(width, block)
    for copy in copies:
        copy.wait()


def local_convolution(own, other, taps, flipped=False, copied=()):
    height, breadth, width = other.shape
    outs = [((height, breadth + 16, width), F32), ((height * breadth, width), F32)]
    outs += [(x.shape, x.dtype) for x in copied]
    scratch = [pltpu.SemaphoreType.DMA((len(copied),))] if copied else []
    return call(
        functools.partial(local_body, flipped, len(copied)),
        outs,
        4.0,
        scratch,
        any_in=tuple(range(3, 3 + len(copied))),
    )(own, other, taps, *copied)


def conv_near_body(near_ref, taps_ref, sum_ref, out_ref, pad_ref):
    c = lax.axis_index("col")
    places, width = sum_ref.shape
    breadth = near_ref.shape[1] // 2
    height, stop = places // breadth, LEFT + breadth
    for core in range(2):

        @pl.when(c == core)
        def _():
            if core == 0:
                pad_ref[:, LEFT : stop + 8, :] = near_ref[:, : breadth + 8, :].astype(F32)
                pad_ref[:, :LEFT, :] = jnp.zeros((3, LEFT, width), F32)
            else:
                pad_ref[:, :stop, :] = near_ref[:, breadth - 8 :, :].astype(F32)
                pad_ref[:, stop : stop + 8, :] = jnp.zeros((3, 8, width), F32)
            first = 0 if core == 0 else height + 3
            lines = [(pad_ref, i, i + first) for i in range(3)]
            for k in range(0, width, 128):
                lanes = slice(k, k + 128)
                sums = [sum_ref[i * breadth : (i + 1) * breadth, lanes] for i in range(height)]
                sums = convolve(lines, sums, taps_ref, breadth, lanes, False)
                for i, row in enumerate(sums):
                    out_ref[i * breadth : (i + 1) * breadth, lanes] = row


def conv_near(near, taps, sums):
    width = sums.shape[1]
    scratch = [pltpu.VMEM((3, near.shape[1] // 2 + 16, width), F32)]
    outs = [(sums.shape, F32)]
    (out,) = call(conv_near_body, outs, 1.5, scratch)(near, taps, sums)
    return out


def conv_norm_body(
    near_ref, far_ref, taps_ref, sum_ref, edge_ref, normed_ref, send_ref, full_ref, inv_ref
):
    places, width = sum_ref.shape
    breadth = near_ref.shape[1] // 2
    height = places // breadth
    steps, half = width // 128, width // 2
    fill_edges(edge_ref, near_ref, far_ref)

    c = lax.axis_index("col")
    for core in range(2):
        lines = edge_lines(edge_ref, height)[3:] if core == 0 else edge_lines(edge_ref, height)[:3]

        @pl.when(c == core)
        def _():
            for k in range(0, width, 128):
                lanes = slice(k, k + 128)
                sums = [sum_ref[i * breadth : (i + 1) * breadth, lanes] for i in range(height)]
                sums = convolve(lines, sums, taps_ref, breadth, lanes, False)
                for i, row in enumerate(sums):
                    full_ref[i * breadth : (i + 1) * breadth, lanes] = row

    for i in range(0, places, 16):
        rows = slice(i, i + 16)
        parts = [full_ref[rows, s * 128 : (s + 1) * 128] for s in range(steps)]
        mean = jnp.sum(functools.reduce(jnp.add, parts), axis=1, keepdims=True) * (1.0 / width)
        parts = [p - mean for p in parts]
        total = functools.reduce(jnp.add, [p * p for p in parts])
        var = jnp.sum(total, axis=1, keepdims=True) * (1.0 / width)
        inv = lax.rsqrt(var + 1e-06)
        inv_ref[rows, :] = jnp.broadcast_to(inv, (16, 128))
        for s, p in enumerate(parts):
            value = p * inv
            full_ref[rows, s * 128 : (s + 1) * 128] = value
            normed_ref[rows, s * 128 : (s + 1) * 128] = value.astype(BF16)
    c = lax.axis_index("col")
    send_ref[...] = normed_ref[:, pl.ds(pl.multiple_of((1 - c) * half, 128), half)]


def conv_norm(near, far, taps, sums):
    places, width = sums.shape
    outs = [
        ((6, near.shape[1] // 2 + 16, width), F32),
        ((places, width), BF16),
        ((places, width // 2), BF16),
        ((places, width), F32),
        ((places, 128), F32),
    ]
    return call(conv_norm_body, outs, 5.0)(near, far, taps, sums)


def lane_pack(rows, stack):
    _, wide = rows.shape
    tall = jnp.concatenate([rows[:, s : s + 128] for s in range(0, wide, 128)], axis=0)
    each = tall.shape[0] // stack
    return jnp.concatenate([tall[s * each : (s + 1) * each] for s in range(stack)], axis=1)


def lane_unpack(packed, n):
    _, wide = packed.shape
    tall = jnp.concatenate([packed[:, s : s + 128] for s in range(0, wide, 128)], axis=0)
    count = tall.shape[0] // n
    return jnp.concatenate([tall[s * n : (s + 1) * n] for s in range(count)], axis=1)


UNITS = 768


def forward_body(
    rows, normed_ref, w_in_ref, w_out_ref, slot_ref, image_ref, scale_ref,
    slope_ref, h_mine_ref, h_send_ref, s_mine_ref, s_send_ref, pre, hidden, branch, block,
):
    c = lax.axis_index("col")
    places, width = branch.shape
    total = w_in_ref.shape[1]
    regions = s_mine_ref.shape[0]
    half = width // 2
    per_chip = total // rows
    per_core = per_chip // 2
    slot = slot_ref[...]
    select = (slot == iota((places, regions), 1).astype(F32)).astype(BF16)
    blocks = total // UNITS

    def expand(f):
        pre[f % 2] = dot(normed_ref[...], w_in_ref[:, f * UNITS : (f + 1) * UNITS])

    def activate(f):
        for row in range(0, places, 16):
            line = slice(row, row + 16)
            for start in range(0, UNITS, 256):
                value = pre[f % 2, line, start : start + 256]
                cdf = 0.5 * (1.0 + lax.erf(value * (1.0 / math.sqrt(2.0))))
                density = jnp.exp(-0.5 * value * value) * (1.0 / math.sqrt(2.0 * math.pi))
                hidden[f % 2, line, start : start + 256] = (value * cdf).astype(BF16)
                at = f * UNITS + start
                slope_ref[line, at : at + 256] = cdf + value * density

    def reduce(f):
        part = dot(hidden[f % 2], w_out_ref[f * UNITS : (f + 1) * UNITS, :])
        branch[...] = part if f == 0 else branch[...] + part
        by_region = dot(hidden[f % 2], select, CONTRACT_ROWS)
        for t in range(UNITS // per_chip):
            q = f * (UNITS // per_chip) + t
            low = by_region[t * per_chip : t * per_chip + per_core]
            high = by_region[t * per_chip + per_core : (t + 1) * per_chip]
            h_mine_ref[q] = lane_pack(jnp.where(c == 0, low, high), half // 128)
            h_send_ref[q] = lane_pack(jnp.where(c == 0, high, low), half // 128).astype(BF16)

    expand(0)
    for f in range(blocks):
        if f + 1 < blocks:
            expand(f + 1)
        activate(f)
        reduce(f)
    block[...] = (image_ref[...].astype(F32) + scale_ref[...] * branch[...]).astype(BF16)
    for at, out in ((c, s_mine_ref), (1 - c, s_send_ref)):
        columns = block[:, pl.ds(pl.multiple_of(at * half, 128), half)]
        out[...] = dot(select, columns, CONTRACT_ROWS)


def mlp_forward(normed, w_in, w_out, slot, image, scale, regions, rows):
    places, width = normed.shape
    total, half = w_in.shape[1], width // 2
    packed = total // rows // 2 * regions // half
    outs = [
        ((places, total), F32),
        ((rows, packed, half), F32),
        ((rows, packed, half), BF16),
        ((regions, half), F32),
        ((regions, half), F32),
    ]
    scratch = [
        pltpu.VMEM((2, places, UNITS), F32),
        pltpu.VMEM((2, places, UNITS), BF16),
        pltpu.VMEM((places, width), F32),
        pltpu.VMEM((places, width), BF16),
    ]
    return call(functools.partial(forward_body, rows), outs, 9.0, scratch, room=12)(
        normed, w_in, w_out, slot, image, scale
    )


def backward_body(
    *refs,
):
    known_refs = refs[:4]
    slot_ref, scale_ref, w_out_ref, slope_ref = refs[4:8]
    g_in_ref, region_ref, dblock_ref, count_ref, g_out, known_all = refs[8:]
    r, c = lax.axis_index("row"), lax.axis_index("col")
    me = 2 * r + c
    places, units = slope_ref.shape
    regions = region_ref.shape[0]
    piece = known_refs[0].shape[0]
    for k in range(4):
        known_all[k * piece : (k + 1) * piece, :] = known_refs[k][...]
    total = 4 * piece
    owned = regions * 8 // total
    known = known_all[...]
    is_count = (iota((total, 128), 0) & 7) == owned
    count = dot(known[:, :regions], is_count.astype(BF16), CONTRACT_ROWS)
    count_ref[...] = count
    line = iota((regions, total), 1)
    bits = (total >> 4).bit_length() - 1
    source = gathered_device(line >> 3, me, bits) * owned + (line & 7)
    place = ((line & 7) < owned) & (source == iota((regions, total), 0))
    pooled = dot(place.astype(BF16), known)
    region_grad = (pooled / (4.0 * count[:, :1])).astype(BF16)
    g_region = (region_grad.astype(F32) * scale_ref[...]).astype(BF16)
    region_ref[...] = g_region
    select = (slot_ref[...] == iota((places, regions), 1).astype(F32)).astype(BF16)
    g_out[...] = dot(select, g_region).astype(BF16)
    dblock_ref[...] = dot(select, region_grad).astype(BF16)

    for f in range(0, units, UNITS):
        at = slice(f, f + UNITS)
        dhidden = dot(g_out[...], w_out_ref[at, :], CONTRACT_LANES)
        g_in_ref[:, at] = (dhidden * slope_ref[:, at]).astype(BF16)


def mlp_backward(known, slot, scale, w_out, slope, regions):
    places, total = slope.shape
    width = w_out.shape[1]
    outs = [
        ((places, total), BF16),
        ((regions, width), BF16),
        ((places, width), BF16),
        ((regions, 128), F32),
    ]
    scratch = [
        pltpu.VMEM((places, width), BF16),
        pltpu.VMEM((4 * known[0].shape[0], width), BF16),
    ]
    return call(backward_body, outs, 4.0, scratch)(
        *known, slot, scale, w_out, slope
    )


def norm_backward_body(g_in_ref, w_in_ref, full_ref, inv_ref, dconv_ref, narrow_ref):
    places, width = dconv_ref.shape
    dconv_ref[...] = dot(g_in_ref[...], w_in_ref[...], CONTRACT_LANES)

    for i in range(0, places, 16):
        rows = slice(i, i + 16)
        lanes = [slice(s, s + 128) for s in range(0, width, 128)]
        grads = [dconv_ref[rows, at] for at in lanes]
        fulls = [full_ref[rows, at] for at in lanes]
        mean = jnp.sum(functools.reduce(jnp.add, grads), axis=1, keepdims=True) * (1.0 / width)
        total = functools.reduce(jnp.add, [g * n for g, n in zip(grads, fulls)])
        along = jnp.sum(total, axis=1, keepdims=True) * (1.0 / width)
        inv = inv_ref[rows, :]
        for at, g, n in zip(lanes, grads, fulls):
            value = inv * (g - mean - n * along)
            dconv_ref[rows, at] = value
            narrow_ref[rows, at] = value.astype(BF16)


def norm_backward(g_in, w_in, full, inv):
    places, width = full.shape
    outs = [((places, width), F32), ((places, width), BF16)]
    return call(norm_backward_body, outs, 4.0)(g_in, w_in, full, inv)


def split_high_low(value):
    high = value.astype(BF16)
    return high, (value - high.astype(F32)).astype(BF16)


CHUNKS = ((0, 256), (256, 128))


def weight_body(
    rows, own_ref, other_ref, normed_ref, normed_other_ref, h_mine_ref, h_got_ref, s_mine_ref,
    s_got_ref, *out_refs,
):
    r, c = lax.axis_index("row"), lax.axis_index("col")
    bits = rows.bit_length() - 1
    half = h_mine_ref.shape[2]
    total = own_ref.shape[1]
    count = rows // 2
    per_chip = total // rows
    packed = h_mine_ref.shape[1]
    per = s_mine_ref.shape[0] // rows
    columns = pl.ds(pl.multiple_of(c * half, 128), half)

    def store(q, value, first):
        for k, (lane, wide) in enumerate(CHUNKS):
            j = layout_place(jnp.int32(q), r, c, orders(bits, k))
            out_refs[2 * k][j, first : first + value.shape[0], :] = value[:, lane : lane + wide]

    for q in range(rows):
        store(q, h_mine_ref[q] + h_got_ref[q].astype(F32), per_chip)
        at = slice(q * per, (q + 1) * per)
        store(q, s_mine_ref[at, :] + s_got_ref[at, :], per_chip + packed)
    for f in range(0, total, UNITS):
        at = slice(f, f + UNITS)
        grad = dot(own_ref[:, at], normed_ref[:, columns], CONTRACT_ROWS)
        grad += dot(other_ref[:, at], normed_other_ref[...], CONTRACT_ROWS)
        for t in range(UNITS // per_chip):
            store((f + t * per_chip) // per_chip, grad[t * per_chip : (t + 1) * per_chip], 0)
    body = per_chip + packed
    for k in range(len(CHUNKS)):
        all_ref, send_ref = out_refs[2 * k : 2 * k + 2]
        for j in range(count):
            send_ref[j, :body, :] = all_ref[count + j, :body, :].astype(BF16)
            send_ref[j, body:, :] = all_ref[count + j, body:, :].astype(BF16)


def weight_gradient(g_in, g_other, normed, normed_other, h_mine, h_got, s_mine, s_got):
    total = g_in.shape[1]
    rows, packed, _ = h_mine.shape
    per = s_mine.shape[0] // rows
    height = total // rows + packed + per
    outs = []
    for _, wide in CHUNKS:
        outs.append(((rows, height, wide), F32))
        outs.append(((rows // 2, height, wide), BF16))
    return call(functools.partial(weight_body, rows), outs, 5.0, room=12)(
        g_in, g_other, normed, normed_other, h_mine, h_got, s_mine, s_got
    )


def merged(keep, got, per):
    body = keep.shape[0] - per
    plain = keep[:body] + got[:body].astype(F32)
    sums = keep[body:] + got[body:].astype(F32)
    return plain, sums


def round_body(per, old_ref, got_ref, keep_ref, send_ref):
    left = keep_ref.shape[0]
    body = keep_ref.shape[1] - per

    def near(i, carry):
        plain, sums = merged(old_ref[i], got_ref[i], per)
        keep_ref[i, :body, :] = plain
        keep_ref[i, body:, :] = sums
        return carry

    def far(i, carry):
        plain, sums = merged(old_ref[i + left], got_ref[i + left], per)
        send_ref[i, :body, :] = plain.astype(BF16)
        send_ref[i, body:, :] = sums.astype(BF16)
        return carry

    lax.fori_loop(0, left, far, 0)
    lax.fori_loop(0, left, near, 0)


def halving_round(keep, got, per):
    _, height, wide = keep.shape
    left = got.shape[0] // 2
    outs = [((left, height, wide), F32), ((left, height, wide), BF16)]
    return call(functools.partial(round_body, per), outs, 0.5)(keep, got)


def taps_to_rows(taps):
    return jnp.concatenate(
        [taps[:, k : k + 128] for k in range(0, taps.shape[1], 128)], axis=0
    )


def rows_to_taps(rows, count):
    pieces = [rows[k : k + count] for k in range(0, rows.shape[0], count)]
    return jnp.concatenate(pieces, axis=1)


def taps_received(got_ref, first, count):
    return rows_to_taps(got_ref[first:, :].astype(F32), count)


def tapped_round_body(
    per, carried, old_ref, got_ref, taps_ref, taps_got_ref, keep_ref, send_ref, taps_out_ref
):
    left = keep_ref.shape[0]
    height = keep_ref.shape[1]
    body = height - per

    def block(i):
        at = pl.ds(pl.multiple_of(i * height, 8), height)
        return merged(old_ref[i], got_ref[at, :], per)

    def near(i, carry):
        plain, sums = block(i)
        keep_ref[i, :body, :] = plain
        keep_ref[i, body:, :] = sums
        return carry

    def far(i, carry):
        plain, sums = block(i + left)
        send_ref[pl.ds(pl.multiple_of(i * height, 8), body), :] = plain.astype(BF16)
        tail = pl.ds(pl.multiple_of(i * height + body, 8), per)
        send_ref[tail, :] = sums.astype(BF16)
        return carry

    lax.fori_loop(0, left, far, 0)
    count = taps_ref.shape[0]
    if carried:
        taps = taps_ref[...] + taps_received(got_ref, 2 * left * height, count)
    else:
        taps = taps_ref[...].astype(F32) + taps_got_ref[...].astype(F32)
    taps_out_ref[...] = taps.astype(BF16).astype(F32)
    send_ref[left * height :, :] = taps_to_rows(taps).astype(BF16)
    lax.fori_loop(0, left, near, 0)


def tapped_round(keep, got, taps, taps_got, left, per):
    _, height, wide = keep.shape
    rows = taps.size // wide
    outs = [
        ((left, height, wide), F32),
        ((left * height + rows, wide), BF16),
        (taps.shape, F32),
    ]
    carried = taps_got is None
    body = functools.partial(tapped_round_body, per, carried)
    return call(body, outs, 0.5)(keep, got.reshape(-1, wide), taps, taps if carried else taps_got)


def finish_body(per, *refs):
    keep_a, got_a, keep_b, got_b, taps_ref, region_ref, count_ref = refs[:7]
    out_ref, mine_ref, send_ref = refs[7:]
    r, c = lax.axis_index("row"), lax.axis_index("col")
    height = keep_b.shape[1]
    done = [merged(keep_a[0], got_a[0], per), merged(keep_b[0], got_b[:height, :], per)]
    plain = jnp.concatenate([d[0] for d in done], axis=1)
    sums = jnp.concatenate([d[1] for d in done], axis=1)
    per_core = out_ref.shape[0]
    half = plain.shape[1]
    first, second = plain[:per_core], plain[per_core : 2 * per_core]
    high, low = split_high_low(lane_unpack(plain[2 * per_core :], per_core))
    out_ref[...] = dot(high, region_ref[...]) + dot(low, region_ref[...])
    mine_ref[:per_core, :] = jnp.where(c == 0, first, second)
    send_ref[:per_core, :] = jnp.where(c == 0, second, first)
    start = pl.multiple_of(r * per, per)
    pooled = sums / (4.0 * count_ref[pl.ds(start, per), :1])
    count = taps_ref.shape[0]
    taps = taps_ref[...] + taps_received(got_b, height, count)
    for ref in (mine_ref, send_ref):
        ref[per_core : per_core + per, :] = pooled
        ref[per_core + per : per_core + per + count, :] = taps[:, :half]
        ref[per_core + per + count :, :] = taps[:, half:]


def finish(parts, taps, region, count, per, per_core):
    width = region.shape[1]
    part = ((per_core + per + 2 * taps.shape[0], width // 2), F32)
    outs = [((per_core, width), F32), part, part]
    return call(functools.partial(finish_body, per), outs, 1.0, far_out=(0,))(
        *parts, taps, region, count
    )


def place_body(per, mine_ref, got_ref, grad_ref, pool_ref, taps_ref):
    c = lax.axis_index("col")
    per_core, width = grad_ref.shape
    half = width // 2
    owned = pool_ref.shape[0]
    first = per_core + per
    count = (mine_ref.shape[0] - first) // 2
    for core in range(2):

        @pl.when(c == core)
        def _():
            left, right = (mine_ref, got_ref) if core == 0 else (got_ref, mine_ref)
            grad_ref[:, :half] = left[:per_core, :]
            grad_ref[:, half:] = right[:per_core, :]
            rows = slice(per_core + core * owned, per_core + (core + 1) * owned)
            pool_ref[:, :half] = left[rows, :]
            pool_ref[:, half:] = right[rows, :]
            for k in range(2):
                at = slice(k * half, (k + 1) * half)
                low = first + k * count
                taps_ref[:28, at] = left[low : low + 28, :]
                taps_ref[28:, at] = right[low : low + 21, :]


def place_outputs(mine, got, per_core, owned, per):
    width = 2 * mine.shape[1]
    outs = [((per_core, width), F32), ((owned, width), F32), ((49, width), F32)]
    return call(functools.partial(place_body, per), outs, 0.5, far_out=(0, 1, 2))(mine, got)


def kernel_gradient_body(pad_ref, edge_ref, dconv_ref, mine_ref, send_ref):
    c = lax.axis_index("col")
    height, wide, width = pad_ref.shape
    breadth = wide - 16

    def block(lanes):
        sums = {}
        grads = [dconv_ref[i * breadth : (i + 1) * breadth, lanes] for i in range(height)]
        for b in range(7):
            start = LEFT - 3 + b
            for ref, at, i in center_lines(pad_ref) + edge_lines(edge_ref, height):
                line = ref[at, start : start + breadth, lanes]
                for a in range(7):
                    row = i - a
                    if 0 <= row < height:
                        term = (line * grads[row]).reshape(breadth // 8, 8, 128).sum(axis=0)
                        sums[a, b] = sums[a, b] + term if (a, b) in sums else term
            for a in range(7):
                sums[a, b] = jnp.sum(sums[a, b], axis=0, keepdims=True)

        def put(ref, first, last):
            ref[24:, lanes] = jnp.zeros((8, 128), F32)
            for a in range(first, last):
                for b in range(7):
                    at = (a - first) * 7 + b
                    ref[at : at + 1, lanes] = sums[a, b]

        @pl.when(c == 0)
        def _():
            put(mine_ref, 0, 4)
            put(send_ref, 4, 7)

        @pl.when(c == 1)
        def _():
            put(mine_ref, 4, 7)
            put(send_ref, 0, 4)

    over_lanes(width, block)


def kernel_gradient(padded, edges, dconv):
    width = dconv.shape[1]
    outs = [((32, width), F32)] * 2
    return call(kernel_gradient_body, outs, 5.0)(padded, edges, dconv)


def back_body(near_ref, far_ref, taps_ref, sum_ref, dblock_ref, out_ref, edge_ref):
    height, breadth, width = out_ref.shape
    fill_edges(edge_ref, near_ref, far_ref)

    def block(lanes):
        sums = [sum_ref[i * breadth : (i + 1) * breadth, lanes] for i in range(height)]
        sums = convolve(edge_lines(edge_ref, height), sums, taps_ref, breadth, lanes, True)
        for i, row in enumerate(sums):
            rows = slice(i * breadth, (i + 1) * breadth)
            out_ref[i, :, lanes] = (dblock_ref[rows, lanes].astype(F32) + row).astype(BF16)

    over_lanes(width, block)


def back_convolution(near, far, taps, sums, dblock):
    places, width = sums.shape
    breadth = near.shape[1] // 2
    outs = [((places // breadth, breadth, width), BF16)]
    scratch = [pltpu.VMEM((6, breadth + 16, width), F32)]
    (out,) = call(back_body, outs, 3.0, scratch, far_out=(0,))(near, far, taps, sums, dblock)
    return out


def gather_stages(bits):
    return list(range((bits - 1) // 2 * 2, -1, -2))


def gather_known(known):
    bits = lax.axis_size("row").bit_length() - 1
    pieces = [known, swap_core(known)]
    for low in gather_stages(bits):
        known = jnp.concatenate(pieces, axis=0)
        pieces = [known]
        for mask in (1 << low, 2 << low, 3 << low):
            pieces.append(exchange(known, (mask, mask)))
    return pieces


def gathered_device(block, me, bits):
    mask = block & 1
    for k, low in enumerate(gather_stages(bits)):
        mask = mask | (((block >> (2 * k + 1)) & 3) << (low + 1))
    return me ^ mask


def compute(image, dw_kernel, w_in, w_out, layer_scale, region_ids, region_slot, pool_grad):
    height, breadth, width = image.shape
    total = w_in.shape[1]
    rows = lax.axis_size("row")
    bits = rows.bit_length() - 1
    regions = region_slot.shape[0]
    owned = pool_grad.shape[0]
    known, slot, own, taps, scale = prepare(
        region_ids, region_slot, pool_grad, image, dw_kernel, layer_scale
    )
    other, near, far = halo(image, own)
    known = gather_known(known)

    padded, sums, w_in, w_out = local_convolution(own, other, taps, copied=(w_in, w_out))
    sums = conv_near(near, taps, sums)
    edges, normed, normed_send, full, inv = conv_norm(near, far, taps, sums)
    normed_other = swap_core(normed_send)
    slope, h_mine, h_send, s_mine, s_send = mlp_forward(
        normed, w_in, w_out, slot, own.reshape(-1, width), scale, regions, rows
    )
    h_got = swap_core(h_send)
    s_got = swap_core(s_send)
    g_in, g_region, dblock, count = mlp_backward(known, slot, scale, w_out, slope, regions)
    g_other = swap_core(g_in)
    dconv, narrow = norm_backward(g_in, w_in, full, inv)
    halves = weight_gradient(g_in, g_other, normed, normed_other, h_mine, h_got, s_mine, s_got)
    per = regions // rows
    part, part_send = kernel_gradient(padded, edges, dconv)
    part = (part + swap_core(part_send)).astype(BF16)
    order = orders(bits, 1)
    part_got = exchange(part, (1 << order[0][0], 1 << order[1][0]))
    parts = []
    for k in range(len(CHUNKS)):
        keep, send = halves[2 * k : 2 * k + 2]
        order = orders(bits, k)
        for step in range(bits):
            got = exchange(send, (1 << order[0][step], 1 << order[1][step]))
            if step == bits - 1:
                break
            if k == 0:
                keep, send = halving_round(keep, got, per)
            else:
                left = rows >> (step + 2)
                keep, send, part = tapped_round(keep, got, part, part_got, left, per)
                part_got = None
        parts += [keep, got]

    narrow = narrow.reshape(height, breadth, width)
    d_other, d_near, d_far = halo(narrow, narrow)
    _, back = local_convolution(dconv, d_other, taps, flipped=True)
    grad_image = back_convolution(d_near, d_far, taps, back, dblock)

    per_core = total // rows // 2
    grad_w_out, mine, send = finish(parts, part, g_region, count, per, per_core)
    got = swap_core(send)
    grad_w_in, region_pool, grad_kernel = place_outputs(mine, got, per_core, owned, per)
    return (region_pool, grad_image, grad_w_in.T, grad_w_out, grad_kernel)


def solution(mesh):
    placed = (
        P(("slides", "row"), "col", None),
        P(),
        P(),
        P(),
        P(),
        P(("slides", "row"), "col"),
        P("slides"),
        P(("slides", "row", "col"), None),
    )
    return jax.shard_map(
        compute,
        mesh=mesh,
        in_specs=placed,
        out_specs=(
            P(("slides", "row", "col"), None),
            P(("slides", "row"), "col", None),
            P("slides", ("row", "col")),
            P(("slides", "row", "col"), None),
            P("slides", None),
        ),
        check_vma=False,
    )
```
